32 devices in a mesh: section: 2 (over x), dp: 4 (over y, core), inner: 4 (over z).
Axes of the slice: x: 2, y: 2, z: 4, core: 2. Of those that a mesh axis runs over, the one named last changes fastest.
Arguments:
- block_io: bfloat16 [2, 32, 320, 768], P('section', ('dp', 'inner')), may hold values from -6 to 6
- segments: int32 [32, 320], P(('dp', 'inner')), may hold values from 0 to 5, as said below
- valid_tokens: int32 [32, 320], P(('dp', 'inner')), may hold values from 0 to 1, as said below
- attention_gain: bfloat16 [2, 768], P('section'), may hold values from 0.5 to 1.5
- attention_shift: bfloat16 [2, 768], P('section'), may hold values from -3 to 3
- triple_weight: bfloat16 [2, 768, 2304], P('section'), may hold values from -0.21875 to 0.21875
- triple_bias: bfloat16 [2, 1536], P('section'), may hold values from -3 to 3
- output_weight: bfloat16 [2, 768, 768], P('section'), may hold values from -1.75 to 1.75
- output_bias: bfloat16 [2, 768], P('section'), may hold values from -3 to 3
- attention_scale: bfloat16 [2, 768], P('section'), may hold values from 0.5 to 1.5
- feed_gain: bfloat16 [2, 768], P('section'), may hold values from 0.5 to 1.5
- feed_shift: bfloat16 [2, 768], P('section'), may hold values from -3 to 3
- up_weight: bfloat16 [2, 768, 3072], P('section'), may hold values from -0.21875 to 0.21875
- up_bias: bfloat16 [2, 3072], P('section'), may hold values from -3 to 3
- down_weight: bfloat16 [2, 3072, 768], P('section'), may hold values from -0.109375 to 0.109375
- down_bias: bfloat16 [2, 768], P('section'), may hold values from -3 to 3
- feed_scale: bfloat16 [2, 768], P('section'), may hold values from 0.5 to 1.5
Outputs:
- block_ends: float32 [2, 32, 320, 768], P('section', ('dp', 'inner'))
- grad_attention_gain: float32 [2, 768], P('section')
- grad_attention_shift: float32 [2, 768], P('section')
- grad_triple_weight: float32 [2, 768, 2304], P('section')
- grad_triple_bias: float32 [2, 1536], P('section')
- grad_output_weight: float32 [2, 768, 768], P('section')
- grad_output_bias: float32 [2, 768], P('section')
- grad_attention_scale: float32 [2, 768], P('section')
- grad_feed_gain: float32 [2, 768], P('section')
- grad_feed_shift: float32 [2, 768], P('section')
- grad_up_weight: float32 [2, 768, 3072], P('section')
- grad_up_bias: float32 [2, 3072], P('section')
- grad_down_weight: float32 [2, 3072, 768], P('section')
- grad_down_bias: float32 [2, 768], P('section')
- grad_feed_scale: float32 [2, 768], P('section')
The draws below stay inside these ranges and needn't reach their ends.
Inputs may be any that keep to these rules, and one draw needn't show every extreme that they name: `segments`: along a packed sequence the segment ids number its images from 0 upward and never fall; padding follows all images of its sequence and carries the id after the last image's. valid_tokens is 1 on image tokens and 0 on the padding at a sequence's end; every sequence starts with an image.
All inputs are finite; a program needn't handle non-finite values.
Results may differ from the reference program's by a relative error of at most 0.0075.
Values may be sent and summed in bfloat16 or wider, within the bound.
A program may use at most 192 MiB of HBM per device.

```python
import math
import jax
import jax.numpy as jnp
from jax import lax

D = 768
HEADS = 12
HEAD = 64
FF = 3072
SEQ = 320
IMG_MIN = 54
IMG_MAX = 261
SEQS = 32


def image_layout(key):
    lengths = jax.random.randint(jax.random.fold_in(key, 11), (SEQS, 6), IMG_MIN, IMG_MAX + 1, dtype=jnp.int32)
    rows = jnp.arange(SEQS, dtype=jnp.int32)
    lengths = jnp.where((rows == 0)[:, None], jnp.int32(IMG_MIN), lengths).astype(jnp.int32)
    finish = jnp.cumsum(lengths, axis=1)
    fitted = finish <= SEQ
    places = jnp.arange(SEQ, dtype=jnp.int32)
    passed = fitted[:, None, :] & (places[None, :, None] >= finish[:, None, :])
    numbers = jnp.sum(passed.astype(jnp.int32), axis=2).astype(jnp.int32)
    filled = jnp.sum(jnp.where(fitted, lengths, 0), axis=1)
    marks = (places[None, :] < filled[:, None]).astype(jnp.int32)
    return (numbers, marks)


def draw_segments(key, part):
    numbers, marks = image_layout(key)
    return numbers


def draw_valid_tokens(key, part):
    numbers, marks = image_layout(key)
    return marks


def block_levels(rng, shape, cuts, least, high):
    def one(axis_at, blocks):
        steps = jax.random.uniform(jax.random.fold_in(jax.random.fold_in(rng, 6), axis_at), (blocks,), jnp.float32, least / len(cuts), high / len(cuts))
        return jnp.repeat(jnp.exp(steps), shape[axis_at] // blocks).reshape((-1,) + (1,) * (len(shape) - axis_at - 1))

    factor_of = one(*cuts[0])
    for cut in cuts[1:]:
        factor_of = factor_of * one(*cut)
    return factor_of


def centred(own_key, dims, scale, reach, shards=(), kind=jnp.bfloat16):
    entries = scale * jax.random.normal(own_key, dims, jnp.float32)
    if shards:
        entries = entries * block_levels(own_key, dims, shards, -0.22, 0.18)
    return jnp.clip(entries, -reach, reach).astype(kind)


def setup_inputs(seed: int = 0) -> dict:
    streams_of = jax.random.split(jax.random.key(seed), 18)
    block_io = centred(streams_of[0], (2, SEQS, SEQ, D), 1.0, 6.0, ((0, 2), (1, 16)))
    segments = draw_segments(jax.random.fold_in(streams_of[17], 71), 0)
    valid_tokens = draw_valid_tokens(jax.random.fold_in(streams_of[17], 71), 0)
    attention_gain = jnp.clip(1.0 + 0.1 * jax.random.normal(streams_of[3], (2, D), jnp.float32), 0.5, 1.5).astype(jnp.bfloat16)
    attention_shift = centred(streams_of[4], (2, D), 0.3, 3.0, ((0, 2),))
    triple_weight = centred(streams_of[5], (2, D, 3 * D), D ** -0.5, 0.21875, ((0, 2),))
    triple_bias = centred(streams_of[6], (2, 2 * D), 0.5, 3.0, ((0, 2),))
    output_weight = centred(streams_of[7], (2, D, D), (D // 64) ** -0.5, 1.75, ((0, 2),))
    output_bias = centred(streams_of[8], (2, D), 0.3, 3.0, ((0, 2),))
    attention_scale = jnp.clip(jnp.exp(math.log(1.5) - 1.0986123 * jax.random.uniform(streams_of[9], (2, D), jnp.float32) ** block_levels(streams_of[9], (2, D), ((0, 2),), -0.2, 0.2)), 0.5, 1.5).astype(jnp.bfloat16)
    feed_gain = jnp.clip(1.0 + 0.1 * jax.random.normal(streams_of[10], (2, D), jnp.float32), 0.5, 1.5).astype(jnp.bfloat16)
    feed_shift = centred(streams_of[11], (2, D), 0.3, 3.0, ((0, 2),))
    up_weight = centred(streams_of[12], (2, D, FF), D ** -0.5, 0.21875, ((0, 2),))
    up_bias = centred(streams_of[13], (2, FF), 0.5, 3.0, ((0, 2),))
    down_weight = centred(streams_of[14], (2, FF, D), FF ** -0.5, 0.109375, ((0, 2),))
    down_bias = centred(streams_of[15], (2, D), 0.3, 3.0, ((0, 2),))
    feed_scale = jnp.clip(jnp.exp(math.log(1.5) - 1.0986123 * jax.random.uniform(streams_of[16], (2, D), jnp.float32) ** block_levels(streams_of[16], (2, D), ((0, 2),), -0.2, 0.2)), 0.5, 1.5).astype(jnp.bfloat16)
    return dict(block_io=block_io, segments=segments, valid_tokens=valid_tokens, attention_gain=attention_gain, attention_shift=attention_shift, triple_weight=triple_weight, triple_bias=triple_bias, output_weight=output_weight, output_bias=output_bias, attention_scale=attention_scale, feed_gain=feed_gain, feed_shift=feed_shift, up_weight=up_weight, up_bias=up_bias, down_weight=down_weight, down_bias=down_bias, feed_scale=feed_scale)


@jax.custom_vjp
def low(v):
    return lax.optimization_barrier(v.astype(jnp.bfloat16)).astype(jnp.float32)

@jax.custom_vjp
def low_back(v):
    return v

def low_keep(v):
    return (low(v), None)

def low_pass(kept, grad):
    return (grad,)

def back_keep(v):
    return (v, None)

def back_low(kept, grad):
    return (low(grad),)
low.defvjp(low_keep, low_pass)
low_back.defvjp(back_keep, back_low)

def layer_norm(values, gain, shift):
    center = values - lax.optimization_barrier(jnp.mean(values, axis=-1, keepdims=True))
    spread = lax.optimization_barrier(jnp.mean(center * center, axis=-1, keepdims=True))
    return center * lax.rsqrt(spread + 1e-06) * gain + shift

def attention_mask(segment_rows, valid_rows):
    same = segment_rows[:, :, None] == segment_rows[:, None, :]
    usable = same & (valid_rows[:, None, :] == 1)
    places = jnp.arange(segment_rows.shape[1], dtype=jnp.int32)
    return usable | (places[:, None] == places[None, :])[None]

def product(left, right):
    return jnp.einsum('bsi,ij->bsj', left, right, precision=lax.Precision.HIGHEST)

def block(block_in, params, allowed):
    attention_gain, attention_shift, triple_weight, triple_bias, output_weight, output_bias, attention_scale, feed_gain, feed_shift, up_weight, up_bias, down_weight, down_bias, feed_scale = params
    count, length, width = block_in.shape
    normed = low(layer_norm(block_in, attention_gain, attention_shift))
    triple_shift = jnp.concatenate([triple_bias[:width], jnp.zeros((width,), jnp.float32), triple_bias[width:]])
    triple = low_back(low(product(normed, triple_weight) + triple_shift))
    query_part = triple[..., :width].reshape(count, length, HEADS, HEAD)
    key_part = triple[..., width:2 * width].reshape(count, length, HEADS, HEAD)
    value_part = triple[..., 2 * width:].reshape(count, length, HEADS, HEAD)
    scores = jnp.einsum('bqhd,bkhd->bhqk', query_part, key_part, precision=lax.Precision.HIGHEST) * HEAD ** (-0.5)
    scores = low_back(jnp.where(allowed[:, None], scores, -1000000000.0))
    probabilities = low(jax.nn.softmax(scores, axis=-1))
    attended = jnp.einsum('bhqk,bkhd->bqhd', probabilities, value_part, precision=lax.Precision.HIGHEST)
    attended = low_back(low(attended.reshape(count, length, width)))
    branch_one = low_back(product(attended, output_weight) + output_bias)
    midway = block_in + attention_scale * branch_one
    normed_two = low(layer_norm(midway, feed_gain, feed_shift))
    hidden_pre = low_back(product(normed_two, up_weight) + up_bias)
    hidden = low(jax.nn.gelu(hidden_pre, approximate=False))
    branch_two = low_back(product(hidden, down_weight) + down_bias)
    return midway + feed_scale * branch_two

def reference(block_io, segments, valid_tokens, attention_gain, attention_shift, triple_weight, triple_bias, output_weight, output_bias, attention_scale, feed_gain, feed_shift, up_weight, up_bias, down_weight, down_bias, feed_scale):
    params = tuple((piece.astype(jnp.float32) for piece in (attention_gain, attention_shift, triple_weight, triple_bias, output_weight, output_bias, attention_scale, feed_gain, feed_shift, up_weight, up_bias, down_weight, down_bias, feed_scale)))
    total = segments.shape[0]
    group = math.gcd(total, 8)
    turns = total // group

    def one_group(carry, index):
        start = (index * group).astype(jnp.int32)
        inputs = lax.dynamic_slice_in_dim(block_io[0], start, group, 0).astype(jnp.float32)
        cotangent = lax.dynamic_slice_in_dim(block_io[1], start, group, 0).astype(jnp.float32)
        allowed = attention_mask(lax.dynamic_slice_in_dim(segments, start, group, 0), lax.dynamic_slice_in_dim(valid_tokens, start, group, 0))

        def whole(entry, weights):
            first_out = block(entry, tuple((piece[0] for piece in weights)), allowed)
            handed = low_back(low(first_out))
            return block(handed, tuple((piece[1] for piece in weights)), allowed)
        result, pull = jax.vjp(whole, inputs, params)
        entry_grad, weight_grads = pull(cotangent)
        carry = tuple((left + right for left, right in zip(carry, weight_grads)))
        return (carry, (result, entry_grad))
    start_carry = tuple((jnp.zeros(piece.shape, jnp.float32) for piece in params))
    sums, (results, entry_grads) = lax.scan(one_group, start_carry, jnp.arange(turns, dtype=jnp.int32))
    shape = block_io.shape[1:]
    block_ends = jnp.stack([entry_grads.reshape(shape), results.reshape(shape)])
    return (block_ends, sums[0], sums[1], sums[2], sums[3], sums[4], sums[5], sums[6], sums[7], sums[8], sums[9], sums[10], sums[11], sums[12], sums[13])
```

```python
import functools

import jax
import jax.numpy as jnp
from jax import lax
from jax.experimental import pallas as pl
from jax.experimental.pallas import tpu as pltpu
from jax.sharding import PartitionSpec as P

HEADS = 12
HEAD = 64
SCALE = HEAD ** (-0.5)
MESH = pl.DeviceIdType.MESH
F32 = jnp.float32
BF16 = jnp.bfloat16
CHUNK = 32
TILE = 256

FWD, DF, DU, DM, ATT, DX, WD, WU, WO, WT = range(10)

TAIL = 0.305
POLY = (
    0.12163973599672318,
    0.12246681749820709,
    0.10342079401016235,
    0.1210220605134964,
    -0.037977732717990875,
    0.18571804463863373,
    -0.15298904478549957,
    0.03669937700033188,
)

NT = (((1,), (1,)), ((), ()))


def nt_dot(left, right):
    return lax.dot_general(left, right, NT, preferred_element_type=F32)


def dot(left, right):
    return jnp.dot(left, right, preferred_element_type=F32)


def ds(start, size, multiple=None):
    if isinstance(start, int):
        return pl.ds(start, size)
    return pl.ds(pl.multiple_of(start, multiple or size), size)


def standardized(values):
    center = values - jnp.mean(values, axis=-1, keepdims=True)
    spread = jnp.mean(center * center, axis=-1, keepdims=True)
    inverse = lax.rsqrt(spread + 1e-06)
    return center * inverse, inverse


def norm_pull(grad, unit, inverse):
    first = jnp.mean(grad, axis=-1, keepdims=True)
    second = jnp.mean(grad * unit, axis=-1, keepdims=True)
    return inverse * (grad - first - unit * second)


def folded(values):
    rows, columns = values.shape
    return jnp.sum(values.reshape(rows // 8, 8, columns), axis=0)


def gelu_pair(values):
    size = jnp.abs(values)
    bell = jnp.exp(-0.5 * values * values)
    t = 1.0 / (1.0 + TAIL * size)
    acc = jnp.full_like(t, POLY[-1])
    for c in POLY[-2::-1]:
        acc = acc * t + c
    tail = acc * t * bell
    phi = jnp.where(values >= 0, 1.0 - tail, tail)
    return values * phi, phi + values * (bell * 0.3989422804014327)


def picked(table, slot):
    value = jnp.int32(table[0])
    for index in range(1, len(table)):
        if table[index] != table[index - 1]:
            value = jnp.where(slot >= index, jnp.int32(table[index]), value)
    return value


def schedules(count):
    parts = (DF, DU, DM, ATT, DX)
    first = [(FWD, m) for m in range(count)]
    for m in range(count - 1):
        first += [(part, m) for part in parts]
    last = count - 1
    first += [(DF, last), (WD, 0), (DU, last), (WU, 0), (DM, last), (WO, 0), (ATT, last), (WT, 0), (DX, last)]
    second = []
    for m in range(count):
        second += [(FWD, m)] + [(part, m) for part in parts]
    second += [(WD, 0), (WU, 0), (WO, 0), (WT, 0)]
    return first, second


def kernel(
    count, length, width, feed,
    data, key_code, query_code, ag, ash, tb, ob, asc, fg, fsh, ub, db, fsc, wt_h, wo_h, wu_h, wd_h,
    ends, gwt, gwo, gwu, gwd, vec,
    wt, wo, wu, wd, x, a, qkv, o, r, m, c, gp, h, f, g, df, dr, tmp, outb, bias, lse, prm, acc, acc_f, acc_t, lhs, stage,
    load_sem, out_sem, stage_sem, send_sem, recv_sem,
):
    section = lax.axis_index("section")
    leading = section == 0
    trailing = section == 1
    pairs = width // 128
    rows_all = count * length
    half = width // 2
    n_chunks = length // CHUNK

    weight_copies = [
        pltpu.make_async_copy(src, dst, load_sem.at[i])
        for i, (src, dst) in enumerate(((wt_h, wt), (wo_h, wo), (wu_h, wu), (wd_h, wd)))
    ]

    def rows_of(mb):
        return ds(mb * length, length, 64)

    def chunk_rows(mb, i):
        return ds(mb * length + i * CHUNK, CHUNK, CHUNK)

    def load_x(i):
        return pltpu.make_async_copy(data.at[i], x.at[pl.ds(i * length, length)], load_sem.at[4 + i])

    def load_g(i):
        return pltpu.make_async_copy(data.at[i], g.at[pl.ds(i * length, length)], load_sem.at[4 + i])

    def handed(mb):
        return pltpu.make_async_remote_copy(
            src_ref=dr.at[rows_of(mb)], dst_ref=x.at[rows_of(mb)],
            send_sem=send_sem.at[mb], recv_sem=recv_sem.at[mb],
            device_id={"section": 1 - section}, device_id_type=MESH,
        )

    def returned(mb):
        return pltpu.make_async_remote_copy(
            src_ref=g.at[rows_of(mb)], dst_ref=g.at[rows_of(mb)],
            send_sem=send_sem.at[mb], recv_sem=recv_sem.at[mb],
            device_id={"section": 1 - section}, device_id_type=MESH,
        )

    def out_copy(mb):
        return pltpu.make_async_copy(outb, ends.at[mb], out_sem)

    @pl.when(leading)
    def _():
        for i in range(count):
            load_x(i).start()

    for copy in weight_copies:
        copy.start()

    @pl.when(trailing)
    def _():
        for i in range(count):
            load_g(i).start()

    barrier = pltpu.get_barrier_semaphore()
    pl.semaphore_signal(barrier, inc=1, device_id={"section": 1 - section}, device_id_type=MESH)

    for row, ref in enumerate((ag, ash, ob, asc, fg, fsh, db, fsc)):
        prm[pl.ds(row, 1), pl.ds(0, width)] = ref[...].astype(F32)
    prm[pl.ds(8, 1), pl.ds(0, width)] = tb[:, pl.ds(0, width)].astype(F32)
    prm[pl.ds(8, 1), pl.ds(width, width)] = jnp.zeros((1, width), F32)
    prm[pl.ds(8, 1), pl.ds(2 * width, width)] = tb[:, pl.ds(width, width)].astype(F32)
    prm[pl.ds(9, 1), :] = ub[...].astype(F32)

    def param(row):
        return prm[pl.ds(row, 1), pl.ds(0, width)]

    acc[...] = jnp.zeros_like(acc)
    acc_f[...] = jnp.zeros_like(acc_f)
    acc_t[...] = jnp.zeros_like(acc_t)

    for i in range(count):
        same = key_code[i] == query_code[i]
        own = lax.broadcasted_iota(jnp.int32, (length, length), 0) == lax.broadcasted_iota(
            jnp.int32, (length, length), 1
        )
        bias[i] = jnp.where(same | own, 0.0, -1000000000.0)

    pl.semaphore_wait(barrier, 1)

    def forward(mb):
        rows = rows_of(mb)

        @pl.when(leading & (mb == 0))
        def _():
            for i in range(count):
                load_x(i).wait()

        @pl.when(trailing)
        def _():
            handed(mb).wait_recv()

        def norm_one(i, carry):
            rr = chunk_rows(mb, i)
            unit, unused = standardized(x[rr, :].astype(F32))
            a[rr, :] = (unit * param(0) + param(1)).astype(BF16)
            return carry

        lax.fori_loop(0, n_chunks, norm_one, 0)

        @pl.when(mb == 0)
        def _():
            weight_copies[0].wait()

        def triple(n, carry):
            cols = ds(n * TILE, TILE)
            qkv[rows, cols] = (dot(a[rows, :], wt[:, cols]) + prm[pl.ds(8, 1), cols]).astype(BF16)
            return carry

        lax.fori_loop(0, 3 * width // TILE, triple, 0)

        lane = lax.broadcasted_iota(jnp.int32, (length, 128), 1) < HEAD

        def attend(p, carry):
            q = qkv[rows, ds(p * 128, 128)]
            k = qkv[rows, ds(width + p * 128, 128)]
            v = qkv[rows, ds(2 * width + p * 128, 128)]
            zero = jnp.zeros_like(q)
            vt = v.T
            outs = []
            for hh in range(2):
                qm = jnp.where(lane, q, zero) if hh == 0 else jnp.where(lane, zero, q)
                s = nt_dot(k, qm) * SCALE + bias[mb]
                top = jnp.max(s, axis=0, keepdims=True)
                e = jnp.exp(s - top)
                total = jnp.sum(e, axis=0, keepdims=True)
                prob = (e * (1.0 / total)).astype(BF16)
                lse[mb, 2 * p + hh] = top + jnp.log(total)
                outs.append(dot(vt[hh * HEAD : (hh + 1) * HEAD], prob))
            o[rows, ds(p * 128, 128)] = jnp.concatenate(outs, axis=0).T.astype(BF16)
            return carry

        lax.fori_loop(0, pairs, attend, 0)

        @pl.when(mb == 0)
        def _():
            weight_copies[1].wait()

        def project(n, carry):
            cols = ds(n * TILE, TILE)
            res = dot(o[rows, :], wo[:, cols]) + prm[pl.ds(2, 1), cols]
            r[rows, cols] = res.astype(BF16)
            m[rows, cols] = x[rows, cols].astype(F32) + prm[pl.ds(3, 1), cols] * res
            return carry

        lax.fori_loop(0, width // TILE, project, 0)

        def norm_two(i, carry):
            rr = chunk_rows(mb, i)
            unit, unused = standardized(m[rr, :])
            c[rr, :] = (unit * param(4) + param(5)).astype(BF16)
            return carry

        lax.fori_loop(0, n_chunks, norm_two, 0)

        @pl.when(mb == 0)
        def _():
            weight_copies[2].wait()

        def up(n, carry):
            cols = ds(n * TILE, TILE)
            u = dot(c[rows, :], wu[:, cols]) + prm[pl.ds(9, 1), cols]
            value, slope = gelu_pair(u)
            h[rows, cols] = value.astype(BF16)
            gp[rows, cols] = slope.astype(BF16)
            return carry

        lax.fori_loop(0, feed // TILE, up, 0)

        @pl.when(mb == 0)
        def _():
            weight_copies[3].wait()

        @pl.when(trailing & (mb > 0))
        def _():
            out_copy(mb - 1).wait()

        def down(n, carry):
            cols = ds(n * TILE, TILE)
            res = dot(h[rows, :], wd[:, cols]) + prm[pl.ds(6, 1), cols]
            f[rows, cols] = res.astype(BF16)
            y = m[rows, cols] + prm[pl.ds(7, 1), cols] * res
            outb[:, cols] = y
            dr[rows, cols] = y.astype(BF16)
            return carry

        lax.fori_loop(0, width // TILE, down, 0)

        @pl.when(leading)
        def _():
            handed(mb).start()

        @pl.when(trailing)
        def _():
            out_copy(mb).start()

    def add_acc(row, values):
        acc[row] += folded(values)

    def grad_f(mb):
        @pl.when(leading)
        def _():
            returned(mb).wait_recv()

        @pl.when(trailing & (mb == 0))
        def _():
            for i in range(count):
                load_g(i).wait()

        def body(i, carry):
            rr = chunk_rows(mb, i)
            up_grad = g[rr, :].astype(F32)
            add_acc(7, up_grad * f[rr, :].astype(F32))
            value = (up_grad * param(7)).astype(BF16)
            df[rr, :] = value
            add_acc(6, value.astype(F32))
            return carry

        lax.fori_loop(0, n_chunks, body, 0)

    def grad_u(mb):
        rows = rows_of(mb)

        def body(n, carry):
            cols = ds(n * TILE, TILE)
            value = (nt_dot(df[rows, :], wd[cols, :]) * gp[rows, cols].astype(F32)).astype(BF16)
            gp[rows, cols] = value
            acc_f[:, cols] += folded(value.astype(F32))
            return carry

        lax.fori_loop(0, feed // TILE, body, 0)

    def grad_m(mb):
        rows = rows_of(mb)

        @pl.when(leading & (mb == 0))
        def _():
            for i in range(count):
                handed(i).wait_send()

        def first(n, carry):
            cols = ds(n * TILE, TILE)
            tmp[:, cols] = nt_dot(gp[rows, :], wu[cols, :])
            return carry

        lax.fori_loop(0, width // TILE, first, 0)

        def body(i, carry):
            rr = chunk_rows(mb, i)
            grad = tmp[ds(i * CHUNK, CHUNK), :]
            unit, inverse = standardized(m[rr, :])
            add_acc(4, grad * unit)
            add_acc(5, grad)
            total = g[rr, :].astype(F32) + norm_pull(grad * param(4), unit, inverse)
            m[rr, :] = total
            add_acc(3, total * r[rr, :].astype(F32))
            value = (total * param(3)).astype(BF16)
            dr[rr, :] = value
            add_acc(2, value.astype(F32))
            return carry

        lax.fori_loop(0, n_chunks, body, 0)

        def second(n, carry):
            cols = ds(n * TILE, TILE)
            g[rows, cols] = nt_dot(dr[rows, :], wo[cols, :]).astype(BF16)
            return carry

        lax.fori_loop(0, width // TILE, second, 0)

    def grad_attend(mb):
        rows = rows_of(mb)
        lane = lax.broadcasted_iota(jnp.int32, (length, 128), 1) < HEAD

        def body(p, carry):
            qc, kc, vc = (ds(part * width + p * 128, 128) for part in range(3))
            q, k, v, do = qkv[rows, qc], qkv[rows, kc], qkv[rows, vc], g[rows, qc]
            zero = jnp.zeros_like(q)
            kt = k.T
            dq = []
            dk = jnp.zeros((length, 128), F32)
            dv = jnp.zeros((length, 128), F32)
            for hh in range(2):
                qm = jnp.where(lane, q, zero) if hh == 0 else jnp.where(lane, zero, q)
                dom = jnp.where(lane, do, zero) if hh == 0 else jnp.where(lane, zero, do)
                s = nt_dot(k, qm) * SCALE + bias[mb]
                prob = jnp.exp(s - lse[mb, 2 * p + hh])
                dv = dv + dot(prob.astype(BF16), dom)
                dp = nt_dot(v, dom)
                inner = jnp.sum(prob * dp, axis=0, keepdims=True)
                grad = (prob * (dp - inner)).astype(BF16)
                dk = dk + dot(grad, qm)
                dq.append(dot(kt[hh * HEAD : (hh + 1) * HEAD], grad))
            dq = (jnp.concatenate(dq, axis=0).T * SCALE).astype(BF16)
            dk = (dk * SCALE).astype(BF16)
            dv = dv.astype(BF16)
            qkv[rows, qc] = dq
            qkv[rows, kc] = dk
            qkv[rows, vc] = dv
            acc_t[:, qc] += folded(dq.astype(F32))
            acc_t[:, vc] += folded(dv.astype(F32))
            return carry

        lax.fori_loop(0, pairs, body, 0)

    def grad_x(mb):
        rows = rows_of(mb)

        def first(n, carry):
            cols = ds(n * TILE, TILE)
            tmp[:, cols] = nt_dot(qkv[rows, :], wt[cols, :])
            return carry

        lax.fori_loop(0, width // TILE, first, 0)

        @pl.when(leading & (mb > 0))
        def _():
            out_copy(mb - 1).wait()

        @pl.when(trailing & (mb == count - 1))
        def _():
            out_copy(mb).wait()

        def body(i, carry):
            rr = chunk_rows(mb, i)
            grad = tmp[ds(i * CHUNK, CHUNK), :]
            unit, inverse = standardized(x[rr, :].astype(F32))
            add_acc(0, grad * unit)
            add_acc(1, grad)
            total = m[rr, :] + norm_pull(grad * param(0), unit, inverse)

            @pl.when(leading)
            def _():
                outb[ds(i * CHUNK, CHUNK), :] = total

            g[rr, :] = total.astype(BF16)
            return carry

        lax.fori_loop(0, n_chunks, body, 0)

        @pl.when(leading)
        def _():
            out_copy(mb).start()

        @pl.when(trailing)
        def _():
            returned(mb).start()

    def weight_grad(left, right, blocks, target, along_rows):
        def body(i, carry):
            block, part = i // 2, i % 2
            if along_rows:
                lhs[...] = left[:, ds(i * half, half)].T
                r0, c0, rc0 = i * half, 0, 0
            else:
                lhs[...] = left[:, ds(part * half, half)].T
                r0, c0, rc0 = part * half, block * width, block * width

            def tile(n, inner):
                cols = ds(n * TILE, TILE)
                stage[:, cols] = dot(lhs[...], right[:, ds(rc0 + n * TILE, TILE)]).astype(BF16)
                return inner

            lax.fori_loop(0, width // TILE, tile, 0)
            copy = pltpu.make_async_copy(
                stage, target.at[ds(r0, half), ds(c0, width, 128)], stage_sem
            )
            copy.start()
            copy.wait()
            return carry

        lax.fori_loop(0, 2 * blocks, body, 0)

    def slot_body(slot, carry):
        one, two = schedules(count)
        phase = jnp.where(leading, picked([e[0] for e in one], slot), picked([e[0] for e in two], slot))
        mb = jnp.where(leading, picked([e[1] for e in one], slot), picked([e[1] for e in two], slot))
        for which, act in ((FWD, forward), (DF, grad_f), (DU, grad_u), (DM, grad_m), (ATT, grad_attend), (DX, grad_x)):
            pl.when(phase == which)(functools.partial(act, mb))
        pl.when(phase == WD)(lambda: weight_grad(h, df, feed // width, gwd, True))
        pl.when(phase == WU)(lambda: weight_grad(c, gp, feed // width, gwu, False))
        pl.when(phase == WO)(lambda: weight_grad(o, dr, 1, gwo, False))
        pl.when(phase == WT)(lambda: weight_grad(a, qkv, 3, gwt, False))
        return carry

    lax.fori_loop(0, len(schedules(count)[0]), slot_body, 0)

    for row in range(8):
        vec[pl.ds(row, 1), pl.ds(0, width)] = jnp.sum(acc[row], axis=0, keepdims=True)
    vec[pl.ds(8, 1), pl.ds(0, 3 * width)] = jnp.sum(acc_t[...], axis=0, keepdims=True)
    vec[pl.ds(9, 1), :] = jnp.sum(acc_f[...], axis=0, keepdims=True)

    @pl.when(leading)
    def _():
        out_copy(count - 1).wait()

    @pl.when(trailing)
    def _():
        for i in range(count):
            returned(i).wait_send()


def local(
    block_io, segments, valid_tokens, attention_gain, attention_shift, triple_weight, triple_bias,
    output_weight, output_bias, attention_scale, feed_gain, feed_shift, up_weight, up_bias,
    down_weight, down_bias, feed_scale,
):
    count, length, width = block_io.shape[1:]
    feed = up_weight.shape[2]
    rows = count * length
    key_code = jnp.where(valid_tokens == 1, segments, -1)[:, :, None]
    query_code = segments[:, None, :]
    any_spec = pl.BlockSpec(memory_space=pl.ANY)
    vmem = pl.BlockSpec(memory_space=pltpu.VMEM)
    outs = pl.pallas_call(
        functools.partial(kernel, count, length, width, feed),
        out_shape=(
            jax.ShapeDtypeStruct((count, length, width), F32),
            jax.ShapeDtypeStruct((width, 3 * width), BF16),
            jax.ShapeDtypeStruct((width, width), BF16),
            jax.ShapeDtypeStruct((width, feed), BF16),
            jax.ShapeDtypeStruct((feed, width), BF16),
            jax.ShapeDtypeStruct((16, feed), F32),
        ),
        in_specs=[any_spec] + [vmem] * 12 + [any_spec] * 4,
        out_specs=(any_spec,) * 5 + (vmem,),
        scratch_shapes=[
            pltpu.VMEM((width, 3 * width), BF16),
            pltpu.VMEM((width, width), BF16),
            pltpu.VMEM((width, feed), BF16),
            pltpu.VMEM((feed, width), BF16),
            pltpu.VMEM((rows, width), BF16),
            pltpu.VMEM((rows, width), BF16),
            pltpu.VMEM((rows, 3 * width), BF16),
            pltpu.VMEM((rows, width), BF16),
            pltpu.VMEM((rows, width), BF16),
            pltpu.VMEM((rows, width), F32),
            pltpu.VMEM((rows, width), BF16),
            pltpu.VMEM((rows, feed), BF16),
            pltpu.VMEM((rows, feed), BF16),
            pltpu.VMEM((rows, width), BF16),
            pltpu.VMEM((rows, width), BF16),
            pltpu.VMEM((rows, width), BF16),
            pltpu.VMEM((rows, width), BF16),
            pltpu.VMEM((length, width), F32),
            pltpu.VMEM((length, width), F32),
            pltpu.VMEM((count, length, length), F32),
            pltpu.VMEM((count, HEADS, 1, length), F32),
            pltpu.VMEM((16, feed), F32),
            pltpu.VMEM((8, 8, width), F32),
            pltpu.VMEM((8, feed), F32),
            pltpu.VMEM((8, 3 * width), F32),
            pltpu.VMEM((width // 2, rows), BF16),
            pltpu.VMEM((width // 2, width), BF16),
            pltpu.SemaphoreType.DMA((4 + count,)),
            pltpu.SemaphoreType.DMA,
            pltpu.SemaphoreType.DMA,
            pltpu.SemaphoreType.DMA((count,)),
            pltpu.SemaphoreType.DMA((count,)),
        ],
        compiler_params=pltpu.CompilerParams(
            collective_id=0, has_side_effects=True, vmem_limit_bytes=62 << 20
        ),
    )(
        block_io[0], key_code, query_code, attention_gain, attention_shift, triple_bias, output_bias,
        attention_scale, feed_gain, feed_shift, up_bias, down_bias, feed_scale,
        triple_weight[0], output_weight[0], up_weight[0], down_weight[0],
    )
    ends, gwt, gwo, gwu, gwd, vec = outs
    gwt, gwo, gwu, gwd, vec = lax.psum((gwt, gwo, gwu, gwd, vec), ("dp", "inner"))

    def row(index):
        return vec[index : index + 1, :width]

    return (
        ends[None],
        row(0),
        row(1),
        gwt.astype(F32)[None],
        jnp.concatenate([vec[8:9, :width], vec[8:9, 2 * width : 3 * width]], axis=1),
        gwo.astype(F32)[None],
        row(2),
        row(3),
        row(4),
        row(5),
        gwu.astype(F32)[None],
        vec[9:10, :],
        gwd.astype(F32)[None],
        row(6),
        row(7),
    )


def solution(mesh):
    split = ("dp", "inner")
    matrix = P("section", None, None)
    vector = P("section", None)
    return jax.shard_map(
        local,
        mesh=mesh,
        in_specs=(
            P("section", split, None, None), P(split, None), P(split, None),
            vector, vector, matrix, vector, matrix, vector, vector, vector, vector,
            matrix, vector, matrix, vector, vector,
        ),
        out_specs=(
            P("section", split, None, None),
            vector, vector, matrix, vector, matrix, vector, vector, vector, vector,
            matrix, vector, matrix, vector, vector,
        ),
        check_vma=False,
    )
```

```python
import functools

import jax
import jax.numpy as jnp
from jax import lax
from jax.experimental import pallas as pl
from jax.experimental.pallas import tpu as pltpu
from jax.sharding import PartitionSpec as P

HEADS = 12
HEAD = 64
SCALE = HEAD ** (-0.5)
MESH = pl.DeviceIdType.MESH
F32 = jnp.float32
BF16 = jnp.bfloat16
CHUNK = 32
TILE = 256

FWD, DF, DU, DM, ATT, DX, WD, WU, WT = range(9)

TAIL = 0.305
POLY = (
    0.12163973599672318,
    0.12246681749820709,
    0.10342079401016235,
    0.1210220605134964,
    -0.037977732717990875,
    0.18571804463863373,
    -0.15298904478549957,
    0.03669937700033188,
)

NT = (((1,), (1,)), ((), ()))


def nt_dot(left, right):
    return lax.dot_general(left, right, NT, preferred_element_type=F32)


def dot(left, right):
    return jnp.dot(left, right, preferred_element_type=F32)


def ds(start, size, multiple=None):
    if isinstance(start, int):
        return pl.ds(start, size)
    return pl.ds(pl.multiple_of(start, multiple or size), size)


def standardized(values):
    center = values - jnp.mean(values, axis=-1, keepdims=True)
    spread = jnp.mean(center * center, axis=-1, keepdims=True)
    inverse = lax.rsqrt(spread + 1e-06)
    return center * inverse, inverse


def norm_pull(grad, unit, inverse):
    first = jnp.mean(grad, axis=-1, keepdims=True)
    second = jnp.mean(grad * unit, axis=-1, keepdims=True)
    return inverse * (grad - first - unit * second)


def folded(values):
    rows, columns = values.shape
    return jnp.sum(values.reshape(rows // 8, 8, columns), axis=0)


def gelu_pair(values):
    size = jnp.abs(values)
    bell = jnp.exp(-0.5 * values * values)
    t = 1.0 / (1.0 + TAIL * size)
    acc = jnp.full_like(t, POLY[-1])
    for c in POLY[-2::-1]:
        acc = acc * t + c
    tail = acc * t * bell
    phi = jnp.where(values >= 0, 1.0 - tail, tail)
    return values * phi, phi + values * (bell * 0.3989422804014327)


def picked(table, slot):
    value = jnp.int32(table[0])
    for index in range(1, len(table)):
        if table[index] != table[index - 1]:
            value = jnp.where(slot >= index, jnp.int32(table[index]), value)
    return value


def schedules(count):
    parts = (DF, DU, DM, ATT, DX)
    first = [(FWD, m) for m in range(count)]
    for m in range(count - 1):
        first += [(part, m) for part in parts]
    last = count - 1
    first += [(DF, last), (WD, 0), (DU, last), (WU, 0), (DM, last), (ATT, last), (WT, 0), (DX, last)]
    second = []
    for m in range(count):
        second += [(FWD, m)] + [(part, m) for part in parts]
    second += [(WD, 0), (WU, 0), (WT, 0)]
    return first, second


def kernel(
    count, length, width, feed, lines, depth, group,
    data, key_code, query_code, ag, ash, tb, ob, asc, fg, fsh, ub, db, fsc, wt_h, wo_h, wu_h, wd_h,
    ends, blocks, vec,
    wt, wo, wu, wd, x, a, qkv, o, r, m, c, gp, h, f, g, df, dr, tmp, outb, bias, lse, prm, acc, acc_f, acc_t, lhs,
    part, twin_part, arrived, vpart, vtwin, varrived,
    load_sem, out_sem, send_sem, recv_sem, stage_send, twin_recv,
    sum_send, sum_recv, all_send, all_recv, pair_send, pair_recv, own_sem,
    vsum_send, vsum_recv, vall_send, vall_recv, vpair_send, vpair_recv,
):
    section = lax.axis_index("section")
    leading = section == 0
    trailing = section == 1
    pairs = width // 128
    rows_all = count * length
    half = width // 2
    n_chunks = length // CHUNK

    weight_copies = [
        pltpu.make_async_copy(src, dst, load_sem.at[i])
        for i, (src, dst) in enumerate(((wt_h, wt), (wo_h, wo), (wu_h, wu), (wd_h, wd)))
    ]

    def rows_of(mb):
        return ds(mb * length, length, 64)

    def chunk_rows(mb, i):
        return ds(mb * length + i * CHUNK, CHUNK, CHUNK)

    def load_x(i):
        return pltpu.make_async_copy(data.at[i], x.at[pl.ds(i * length, length)], load_sem.at[4 + i])

    def load_g(i):
        return pltpu.make_async_copy(data.at[i], g.at[pl.ds(i * length, length)], load_sem.at[4 + i])

    def handed(mb):
        return pltpu.make_async_remote_copy(
            src_ref=dr.at[rows_of(mb)], dst_ref=x.at[rows_of(mb)],
            send_sem=send_sem.at[mb], recv_sem=recv_sem.at[mb],
            device_id={"section": 1 - section}, device_id_type=MESH,
        )

    def returned(mb):
        return pltpu.make_async_remote_copy(
            src_ref=g.at[rows_of(mb)], dst_ref=g.at[rows_of(mb)],
            send_sem=send_sem.at[mb], recv_sem=recv_sem.at[mb],
            device_id={"section": 1 - section}, device_id_type=MESH,
        )

    def out_copy(mb):
        return pltpu.make_async_copy(outb, ends.at[mb], out_sem)

    @pl.when(leading)
    def _():
        for i in range(count):
            load_x(i).start()

    for copy in weight_copies:
        copy.start()

    @pl.when(trailing)
    def _():
        for i in range(count):
            load_g(i).start()

    dp, z = lax.axis_index("dp"), lax.axis_index("inner")
    core, y = dp % 2, dp // 2
    ring = lines * depth
    place = y * depth + jnp.where(y % 2 == 0, z, depth - 1 - z)

    def ring_device(index):
        index = lax.rem(index + ring, ring)
        row, along = index // depth, index % depth
        return {"dp": row * 2 + core, "inner": jnp.where(row % 2 == 0, along, depth - 1 - along)}

    neighbours = (ring_device(place + 1), ring_device(place - 1))
    sibling = {"dp": y * 2 + 1 - core}

    barrier = pltpu.get_barrier_semaphore()
    for device in ({"section": 1 - section}, sibling) + neighbours:
        pl.semaphore_signal(barrier, inc=1, device_id=device, device_id_type=MESH)

    for row, ref in enumerate((ag, ash, ob, asc, fg, fsh, db, fsc)):
        prm[pl.ds(row, 1), pl.ds(0, width)] = ref[...].astype(F32)
    prm[pl.ds(8, 1), pl.ds(0, width)] = tb[:, pl.ds(0, width)].astype(F32)
    prm[pl.ds(8, 1), pl.ds(width, width)] = jnp.zeros((1, width), F32)
    prm[pl.ds(8, 1), pl.ds(2 * width, width)] = tb[:, pl.ds(width, width)].astype(F32)
    prm[pl.ds(9, 1), :] = ub[...].astype(F32)

    def param(row):
        return prm[pl.ds(row, 1), pl.ds(0, width)]

    acc[...] = jnp.zeros_like(acc)
    acc_f[...] = jnp.zeros_like(acc_f)
    acc_t[...] = jnp.zeros_like(acc_t)

    for i in range(count):
        same = key_code[i] == query_code[i]
        own = lax.broadcasted_iota(jnp.int32, (length, length), 0) == lax.broadcasted_iota(
            jnp.int32, (length, length), 1
        )
        bias[i] = jnp.where(same | own, 0.0, -1000000000.0)

    pl.semaphore_wait(barrier, 4)

    lane = lax.broadcasted_iota(jnp.int32, (length, 128), 1) < HEAD

    def norm_one(mb):
        def body(i, carry):
            rr = chunk_rows(mb, i)
            unit, unused = standardized(x[rr, :].astype(F32))
            a[rr, :] = (unit * param(0) + param(1)).astype(BF16)
            return carry

        lax.fori_loop(0, n_chunks, body, 0)

    def triple(mb):
        rows = rows_of(mb)

        def body(n, carry):
            cols = ds(n * TILE, TILE)
            qkv[rows, cols] = (dot(a[rows, :], wt[:, cols]) + prm[pl.ds(8, 1), cols]).astype(BF16)
            return carry

        lax.fori_loop(0, 3 * width // TILE, body, 0)

    def attend(mb):
        rows = rows_of(mb)

        def body(p, carry):
            q = qkv[rows, ds(p * 128, 128)]
            k = qkv[rows, ds(width + p * 128, 128)]
            v = qkv[rows, ds(2 * width + p * 128, 128)]
            zero = jnp.zeros_like(q)
            vt = v.T
            outs = []
            for hh in range(2):
                qm = jnp.where(lane, q, zero) if hh == 0 else jnp.where(lane, zero, q)
                s = nt_dot(k, qm) * SCALE + bias[mb]
                top = jnp.max(s, axis=0, keepdims=True)
                e = jnp.exp(s - top)
                total = jnp.sum(e, axis=0, keepdims=True)
                prob = (e * (1.0 / total)).astype(BF16)
                lse[mb, 2 * p + hh] = top + jnp.log(total)
                outs.append(dot(vt[hh * HEAD : (hh + 1) * HEAD], prob))
            o[rows, ds(p * 128, 128)] = jnp.concatenate(outs, axis=0).T.astype(BF16)
            return carry

        lax.fori_loop(0, pairs, body, 0)

    def project(mb):
        rows = rows_of(mb)

        def body(n, carry):
            cols = ds(n * TILE, TILE)
            res = dot(o[rows, :], wo[:, cols]) + prm[pl.ds(2, 1), cols]
            r[rows, cols] = res.astype(BF16)
            m[rows, cols] = x[rows, cols].astype(F32) + prm[pl.ds(3, 1), cols] * res
            return carry

        lax.fori_loop(0, width // TILE, body, 0)

    def norm_two(mb):
        def body(i, carry):
            rr = chunk_rows(mb, i)
            unit, unused = standardized(m[rr, :])
            c[rr, :] = (unit * param(4) + param(5)).astype(BF16)
            return carry

        lax.fori_loop(0, n_chunks, body, 0)

    def up(mb):
        rows = rows_of(mb)

        def body(n, carry):
            cols = ds(n * TILE, TILE)
            u = dot(c[rows, :], wu[:, cols]) + prm[pl.ds(9, 1), cols]
            value, slope = gelu_pair(u)
            h[rows, cols] = value.astype(BF16)
            gp[rows, cols] = slope.astype(BF16)
            return carry

        lax.fori_loop(0, feed // TILE, body, 0)

    def down(mb):
        rows = rows_of(mb)

        def body(n, carry):
            cols = ds(n * TILE, TILE)
            res = dot(h[rows, :], wd[:, cols]) + prm[pl.ds(6, 1), cols]
            f[rows, cols] = res.astype(BF16)
            y = m[rows, cols] + prm[pl.ds(7, 1), cols] * res
            outb[:, cols] = y
            dr[rows, cols] = y.astype(BF16)
            return carry

        lax.fori_loop(0, width // TILE, body, 0)

    def forward(mb):
        def when_first(act):
            pl.when(mb == 0)(act)

        @pl.when(leading & (mb == 0))
        def _():
            for i in range(count):
                load_x(i).wait()

        @pl.when(trailing)
        def _():
            handed(mb).wait_recv()

        norm_one(mb)
        when_first(weight_copies[0].wait)
        triple(mb)
        attend(mb)
        when_first(weight_copies[1].wait)
        project(mb)
        norm_two(mb)
        when_first(weight_copies[2].wait)
        up(mb)
        when_first(weight_copies[3].wait)

        @pl.when(trailing & (mb > 0))
        def _():
            out_copy(mb - 1).wait()

        down(mb)

        @pl.when(leading)
        def _():
            handed(mb).start()

        @pl.when(trailing)
        def _():
            out_copy(mb).start()

    def add_acc(row, values):
        acc[row] += folded(values)

    def grad_f(mb):
        @pl.when(leading)
        def _():
            returned(mb).wait_recv()

        @pl.when(trailing & (mb == 0))
        def _():
            for i in range(count):
                load_g(i).wait()

        def body(i, carry):
            rr = chunk_rows(mb, i)
            up_grad = g[rr, :].astype(F32)
            add_acc(7, up_grad * f[rr, :].astype(F32))
            value = (up_grad * param(7)).astype(BF16)
            df[rr, :] = value
            add_acc(6, value.astype(F32))
            return carry

        lax.fori_loop(0, n_chunks, body, 0)

    def grad_u(mb):
        rows = rows_of(mb)

        def body(n, carry):
            cols = ds(n * TILE, TILE)
            value = (nt_dot(df[rows, :], wd[cols, :]) * gp[rows, cols].astype(F32)).astype(BF16)
            gp[rows, cols] = value
            acc_f[:, cols] += folded(value.astype(F32))
            return carry

        lax.fori_loop(0, feed // TILE, body, 0)

    def grad_m(mb):
        rows = rows_of(mb)

        @pl.when(leading & (mb == 0))
        def _():
            for i in range(count):
                handed(i).wait_send()

        def first(n, carry):
            cols = ds(n * TILE, TILE)
            tmp[:, cols] = nt_dot(gp[rows, :], wu[cols, :])
            return carry

        lax.fori_loop(0, width // TILE, first, 0)

        def body(i, carry):
            rr = chunk_rows(mb, i)
            grad = tmp[ds(i * CHUNK, CHUNK), :]
            unit, inverse = standardized(m[rr, :])
            add_acc(4, grad * unit)
            add_acc(5, grad)
            total = g[rr, :].astype(F32) + norm_pull(grad * param(4), unit, inverse)
            m[rr, :] = total
            add_acc(3, total * r[rr, :].astype(F32))
            value = (total * param(3)).astype(BF16)
            dr[rr, :] = value
            add_acc(2, value.astype(F32))
            return carry

        lax.fori_loop(0, n_chunks, body, 0)

        def second(n, carry):
            cols = ds(n * TILE, TILE)
            g[rows, cols] = nt_dot(dr[rows, :], wo[cols, :]).astype(BF16)
            return carry

        lax.fori_loop(0, width // TILE, second, 0)

    def grad_attend(mb):
        rows = rows_of(mb)

        def body(p, carry):
            qc, kc, vc = (ds(part * width + p * 128, 128) for part in range(3))
            q, k, v, do = qkv[rows, qc], qkv[rows, kc], qkv[rows, vc], g[rows, qc]
            zero = jnp.zeros_like(q)
            kt = k.T
            dq = []
            dk = jnp.zeros((length, 128), F32)
            dv = jnp.zeros((length, 128), F32)
            for hh in range(2):
                qm = jnp.where(lane, q, zero) if hh == 0 else jnp.where(lane, zero, q)
                dom = jnp.where(lane, do, zero) if hh == 0 else jnp.where(lane, zero, do)
                s = nt_dot(k, qm) * SCALE + bias[mb]
                prob = jnp.exp(s - lse[mb, 2 * p + hh])
                dv = dv + dot(prob.astype(BF16), dom)
                dp = nt_dot(v, dom)
                inner = jnp.sum(prob * dp, axis=0, keepdims=True)
                grad = (prob * (dp - inner)).astype(BF16)
                dk = dk + dot(grad, qm)
                dq.append(dot(kt[hh * HEAD : (hh + 1) * HEAD], grad))
            dq = (jnp.concatenate(dq, axis=0).T * SCALE).astype(BF16)
            dk = (dk * SCALE).astype(BF16)
            dv = dv.astype(BF16)
            qkv[rows, qc] = dq
            qkv[rows, kc] = dk
            qkv[rows, vc] = dv
            acc_t[:, qc] += folded(dq.astype(F32))
            acc_t[:, vc] += folded(dv.astype(F32))
            return carry

        lax.fori_loop(0, pairs, body, 0)

    def grad_x(mb):
        rows = rows_of(mb)

        def first(n, carry):
            cols = ds(n * TILE, TILE)
            tmp[:, cols] = nt_dot(qkv[rows, :], wt[cols, :])
            return carry

        lax.fori_loop(0, width // TILE, first, 0)

        @pl.when(leading & (mb > 0))
        def _():
            out_copy(mb - 1).wait()

        @pl.when(trailing & (mb == count - 1))
        def _():
            out_copy(mb).wait()

        def body(i, carry):
            rr = chunk_rows(mb, i)
            grad = tmp[ds(i * CHUNK, CHUNK), :]
            unit, inverse = standardized(x[rr, :].astype(F32))
            add_acc(0, grad * unit)
            add_acc(1, grad)
            total = m[rr, :] + norm_pull(grad * param(0), unit, inverse)

            @pl.when(leading)
            def _():
                outb[ds(i * CHUNK, CHUNK), :] = total

            g[rr, :] = total.astype(BF16)
            return carry

        lax.fori_loop(0, n_chunks, body, 0)

        @pl.when(leading)
        def _():
            out_copy(mb).start()

        @pl.when(trailing)
        def _():
            returned(mb).start()

    n_blocks = (3 * width + width + 2 * feed) // width
    pieces = n_blocks // group
    piece_rows = group * half
    chunk = piece_rows // ring
    staged = n_blocks * half

    def remote(src, dst, send, recv, device):
        return pltpu.make_async_remote_copy(
            src_ref=src, dst_ref=dst, send_sem=send, recv_sem=recv, device_id=device, device_id_type=MESH
        )

    def twin_copy(block, slot):
        return remote(
            part.at[ds(staged + slot * half, half, 16)], twin_part.at[ds(block * half, half, 16)],
            stage_send.at[slot], twin_recv.at[block], sibling,
        )

    def half_block(index, source):
        piece, turn = index // (2 * group), index % (2 * group)
        away = turn < group
        block = piece * group + turn % group
        slot = turn % 2
        side = jnp.where(away, 1 - core, core)
        base = pl.multiple_of(jnp.where(away, staged + slot * half, block * half), 16)

        @pl.when(away & ((piece > 0) | (turn > 1)))
        def _():
            twin_copy(block, slot).wait_send()

        source(block, side, base)

        @pl.when(away)
        def _():
            twin_copy(block, slot).start()

    def product(left, right, left_start, right_start, base):
        lhs[...] = left[:, ds(left_start, half, 128)].T

        def tile(n, inner):
            part[pl.ds(base, half), ds(n * TILE, TILE)] = dot(
                lhs[...], right[:, ds(right_start + n * TILE, TILE)]
            ).astype(BF16)
            return inner

        lax.fori_loop(0, width // TILE, tile, 0)

    per = feed // width

    def from_down(block, side, base):
        product(h, df, block * width + side * half, 0, base)

    def from_up(block, side, base):
        product(c, gp, side * half, (block - per) * width, base)

    def from_rest(block, side, base):
        pl.when(block == 2 * per)(lambda: product(o, dr, side * half, 0, base))
        pl.when(block > 2 * per)(lambda: product(a, qkv, side * half, (block - 2 * per - 1) * width, base))

    halves = 2 * per
    first_tick = 2 * group

    def weight_grad(phase, source):
        def body(i, carry):
            index = phase * halves + i

            @pl.when(index >= first_tick)
            def _():
                tick(index - first_tick)

            half_block(index, source)
            return carry

        lax.fori_loop(0, halves, body, 0)

    def where_rows(k, j):
        return ds(k * piece_rows + j * chunk, chunk, 16)

    def where_out(k, j):
        offset = k * piece_rows + j * chunk
        return ds((offset // half) * width + core * half + offset % half, chunk, 16)

    def wrapped(index):
        return lax.rem(index + 2 * ring, ring)

    def sum_copy(k, d, s, j):
        index = (k * 2 + d) * (ring - 1) + s
        return remote(
            part.at[where_rows(k, j), pl.ds(d * half, half)], arrived.at[index],
            sum_send.at[index], sum_recv.at[index], neighbours[d],
        )

    def all_copy(k, d, s, j):
        index = (k * 2 + d) * (ring - 1) + s
        there = blocks.at[where_out(k, j), pl.ds(d * half, half)]
        return remote(there, there, all_send.at[index], all_recv.at[index], neighbours[d])

    def all_first(k, d, j):
        index = (k * 2 + d) * (ring - 1)
        return remote(
            part.at[where_rows(k, j), pl.ds(d * half, half)], blocks.at[where_out(k, j), pl.ds(d * half, half)],
            all_send.at[index], all_recv.at[index], neighbours[d],
        )

    def pair_copy(k, d, src, j):
        index = k * 2 + d
        return remote(
            src, blocks.at[where_out(k, j), pl.ds(d * half, half)], pair_send.at[index], pair_recv.at[index], sibling
        )

    def own_copy(k, d, j):
        return pltpu.make_async_copy(
            part.at[where_rows(k, j), pl.ds(d * half, half)], blocks.at[where_out(k, j), pl.ds(d * half, half)],
            own_sem.at[k * 2 + d],
        )

    def piece_event(k, e):
        @pl.when(e == 0)
        def _():
            for b in range(group):
                twin_copy(k * group + b, 0).wait_recv()

            def combine(i, carry):
                rr = ds(k * piece_rows + i * CHUNK, CHUNK)
                part[rr, :] = (part[rr, :].astype(F32) + twin_part[rr, :].astype(F32)).astype(BF16)
                return carry

            lax.fori_loop(0, piece_rows // CHUNK, combine, 0)
            for d in range(2):
                sum_copy(k, d, 0, place).start()

        @pl.when((e > 0) & (e < ring))
        def _():
            s = e - 1
            for d, sign in ((0, 1), (1, -1)):
                j = wrapped(place - sign * (s + 1))
                sum_copy(k, d, s, j).wait_recv()
                rr, cols = where_rows(k, j), pl.ds(d * half, half)
                total = part[rr, cols].astype(F32) + arrived[(k * 2 + d) * (ring - 1) + s].astype(F32)
                part[rr, cols] = total.astype(BF16)

                @pl.when(e < ring - 1)
                def _():
                    sum_copy(k, d, e, j).start()

                @pl.when(e == ring - 1)
                def _():
                    all_first(k, d, j).start()
                    pair_copy(k, d, part.at[rr, cols], j).start()
                    own_copy(k, d, j).start()

        @pl.when(e >= ring)
        def _():
            s = e - ring
            for d, sign in ((0, 1), (1, -1)):
                j = wrapped(place - sign * s)
                all_copy(k, d, s, j).wait_recv()

                @pl.when(s < ring - 2)
                def _():
                    all_copy(k, d, s + 1, j).start()

                pair_copy(k, d, blocks.at[where_out(k, j), pl.ds(d * half, half)], j).start()

    events = 2 * ring - 1

    def tick(t):
        def body(k, carry):
            e = t - k * 2 * group
            pl.when((e >= 0) & (e < events))(lambda: piece_event(k, e))
            return carry

        lax.fori_loop(0, pieces, body, 0)

    vhalf = ring * 8

    def vrows(j):
        return ds(core * vhalf + j * 8, 8)

    def vpair_copy():
        return remote(vpart.at[ds((1 - core) * vhalf, vhalf)], vtwin, vpair_send.at[0], vpair_recv.at[0], sibling)

    def vsum_copy(s, j):
        return remote(vpart.at[vrows(j)], varrived.at[s], vsum_send.at[s], vsum_recv.at[s], neighbours[0])

    def vall_copy(s, j, src):
        return remote(src.at[vrows(j)], vec.at[vrows(j)], vall_send.at[s], vall_recv.at[s], neighbours[0])

    def vout_copy(src, rr):
        return remote(src.at[rr], vec.at[rr], vpair_send.at[1], vpair_recv.at[1], sibling)

    def vector_event(e):
        @pl.when(e == 0)
        def _():
            vpair_copy().start()
            vpair_copy().wait_recv()
            rr = ds(core * vhalf, vhalf)
            vpart[rr, :] = vpart[rr, :] + vtwin[...]
            vsum_copy(0, place).start()

        @pl.when((e > 0) & (e < ring))
        def _():
            j = wrapped(place - e)
            vsum_copy(e - 1, j).wait_recv()
            rr = vrows(j)
            vpart[rr, :] = vpart[rr, :] + varrived[e - 1]

            @pl.when(e < ring - 1)
            def _():
                vsum_copy(e, j).start()

            @pl.when(e == ring - 1)
            def _():
                vec[rr, :] = vpart[rr, :]
                vall_copy(0, j, vpart).start()

        @pl.when(e >= ring)
        def _():
            s = e - ring
            j = wrapped(place - s)
            vall_copy(s, j, vec).wait_recv()

            @pl.when(s < ring - 2)
            def _():
                vall_copy(s + 1, j, vec).start()

            @pl.when(s == ring - 2)
            def _():
                vout_copy(vec, ds(core * vhalf, vhalf)).start()

    def pack_vectors():
        vpart[...] = jnp.zeros_like(vpart)
        at = 0
        for ref, size in [(acc.at[row], width) for row in range(8)] + [(acc_t, 3 * width), (acc_f, feed)]:
            for i in range(size // 128):
                vpart[pl.ds(at, 1), :] = jnp.sum(ref[:, pl.ds(i * 128, 128)], axis=0, keepdims=True)
                at += 1

    def finish():
        for d in range(2):
            def body(k, carry):
                whole = blocks.at[ds(k * piece_rows, piece_rows, 16), pl.ds(d * half, half)]
                index = k * 2 + d
                remote(whole, whole, pair_send.at[index], pair_recv.at[index], sibling).wait()
                own_copy(k, d, 0).wait()

                def sends(s, inner):
                    sum_copy(k, d, s, 0).wait_send()
                    all_copy(k, d, s, 0).wait_send()
                    return inner

                return lax.fori_loop(0, ring - 1, sends, carry)

            lax.fori_loop(0, pieces, body, 0)

        def vsends(s, carry):
            vsum_copy(s, 0).wait_send()
            vall_copy(s, 0, vec).wait_send()
            return carry

        lax.fori_loop(0, ring - 1, vsends, 0)
        vpair_copy().wait_send()
        vout_copy(vec, ds(core * vhalf, vhalf)).wait_send()
        vout_copy(vec, ds((1 - core) * vhalf, vhalf)).wait_recv()
        for slot in range(2):
            twin_copy(0, slot).wait_send()

    def slot_body(slot, carry):
        one, two = schedules(count)
        phase = jnp.where(leading, picked([e[0] for e in one], slot), picked([e[0] for e in two], slot))
        mb = jnp.where(leading, picked([e[1] for e in one], slot), picked([e[1] for e in two], slot))
        for which, act in ((FWD, forward), (DF, grad_f), (DU, grad_u), (DM, grad_m), (ATT, grad_attend), (DX, grad_x)):
            pl.when(phase == which)(functools.partial(act, mb))
        for number, (which, source) in enumerate(((WD, from_down), (WU, from_up), (WT, from_rest))):
            pl.when(phase == which)(functools.partial(weight_grad, number, source))
        return carry

    lax.fori_loop(0, len(schedules(count)[0]), slot_body, 0)
    pack_vectors()

    last_tick = (pieces - 1) * 2 * group + events
    start_tick = 2 * n_blocks - first_tick

    def drain(t, carry):
        tick(t)
        e = t - start_tick - 1
        pl.when((e >= 0) & (e < events))(lambda: vector_event(e))
        return carry

    lax.fori_loop(start_tick, max(last_tick, start_tick + 1 + events), drain, 0)
    finish()

    @pl.when(leading)
    def _():
        out_copy(count - 1).wait()

    @pl.when(trailing)
    def _():
        for i in range(count):
            returned(i).wait_send()


def widen_kernel(per, source, gwd, gwu, gwo, gwt):
    block = pl.program_id(0)
    for target, first, after in ((gwd, 0, per), (gwu, per, 2 * per), (gwo, 2 * per, 2 * per + 1), (gwt, 2 * per + 1, 2 * per + 4)):

        @pl.when((block >= first) & (block < after))
        def _():
            target[...] = source[...].astype(F32)


def widened(blocks, width, per):
    half = width // 2

    def rows_down(i, part):
        return (jnp.where(i < per, 2 * i + part, 2 * per - 1), 0)

    def beside(first, number):
        def index(i, part):
            inside = jnp.clip(i - first, 0, number - 1)
            side = jnp.where(i < first, 0, jnp.where(i >= first + number, 1, part))
            return (side, inside)

        return index

    shape = (half, width)
    return pl.pallas_call(
        functools.partial(widen_kernel, per),
        grid=(2 * per + 4, 2),
        in_specs=[pl.BlockSpec(shape, lambda i, part: (2 * i + part, 0))],
        out_specs=(
            pl.BlockSpec(shape, rows_down),
            pl.BlockSpec(shape, beside(per, per)),
            pl.BlockSpec(shape, beside(2 * per, 1)),
            pl.BlockSpec(shape, beside(2 * per + 1, 3)),
        ),
        out_shape=(
            jax.ShapeDtypeStruct((per * width, width), F32),
            jax.ShapeDtypeStruct((width, per * width), F32),
            jax.ShapeDtypeStruct((width, width), F32),
            jax.ShapeDtypeStruct((width, 3 * width), F32),
        ),
        compiler_params=pltpu.CompilerParams(vmem_limit_bytes=60 << 20),
    )(blocks)


def local(
    block_io, segments, valid_tokens, attention_gain, attention_shift, triple_weight, triple_bias,
    output_weight, output_bias, attention_scale, feed_gain, feed_shift, up_weight, up_bias,
    down_weight, down_bias, feed_scale,
):
    count, length, width = block_io.shape[1:]
    feed = up_weight.shape[2]
    rows = count * length
    half = width // 2
    lines, depth = lax.axis_size("dp") // 2, lax.axis_size("inner")
    ring = lines * depth
    n_blocks = (4 * width + 2 * feed) // width
    group = 2 if (2 * half) % (16 * ring) == 0 else feed // width
    pieces = n_blocks // group
    streams = pieces * 2 * (ring - 1)
    chunk = group * half // ring
    key_code = jnp.where(valid_tokens == 1, segments, -1)[:, :, None]
    query_code = segments[:, None, :]
    any_spec = pl.BlockSpec(memory_space=pl.ANY)
    vmem = pl.BlockSpec(memory_space=pltpu.VMEM)
    sem = pltpu.SemaphoreType.DMA
    ends, blocks, vec = pl.pallas_call(
        functools.partial(kernel, count, length, width, feed, lines, depth, group),
        out_shape=(
            jax.ShapeDtypeStruct((count, length, width), F32),
            jax.ShapeDtypeStruct((n_blocks * width, width), BF16),
            jax.ShapeDtypeStruct((2 * ring * 8, 128), F32),
        ),
        in_specs=[any_spec] + [vmem] * 12 + [any_spec] * 4,
        out_specs=(any_spec, any_spec, vmem),
        scratch_shapes=[
            pltpu.VMEM((width, 3 * width), BF16),
            pltpu.VMEM((width, width), BF16),
            pltpu.VMEM((width, feed), BF16),
            pltpu.VMEM((feed, width), BF16),
            pltpu.VMEM((rows, width), BF16),
            pltpu.VMEM((rows, width), BF16),
            pltpu.VMEM((rows, 3 * width), BF16),
            pltpu.VMEM((rows, width), BF16),
            pltpu.VMEM((rows, width), BF16),
            pltpu.VMEM((rows, width), F32),
            pltpu.VMEM((rows, width), BF16),
            pltpu.VMEM((rows, feed), BF16),
            pltpu.VMEM((rows, feed), BF16),
            pltpu.VMEM((rows, width), BF16),
            pltpu.VMEM((rows, width), BF16),
            pltpu.VMEM((rows, width), BF16),
            pltpu.VMEM((rows, width), BF16),
            pltpu.VMEM((length, width), F32),
            pltpu.VMEM((length, width), F32),
            pltpu.VMEM((count, length, length), F32),
            pltpu.VMEM((count, HEADS, 1, length), F32),
            pltpu.VMEM((16, feed), F32),
            pltpu.VMEM((8, 8, width), F32),
            pltpu.VMEM((8, feed), F32),
            pltpu.VMEM((8, 3 * width), F32),
            pltpu.VMEM((half, rows), BF16),
            pltpu.VMEM((n_blocks * half + 2 * half, width), BF16),
            pltpu.VMEM((n_blocks * half, width), BF16),
            pltpu.VMEM((streams, chunk, half), BF16),
            pltpu.VMEM((2 * ring * 8, 128), F32),
            pltpu.VMEM((ring * 8, 128), F32),
            pltpu.VMEM((ring - 1, 8, 128), F32),
            sem((4 + count,)),
            sem,
            sem((count,)),
            sem((count,)),
            sem((2,)),
            sem((n_blocks,)),
            sem((streams,)),
            sem((streams,)),
            sem((streams,)),
            sem((streams,)),
            sem((2 * pieces,)),
            sem((2 * pieces,)),
            sem((2 * pieces,)),
            sem((ring - 1,)),
            sem((ring - 1,)),
            sem((ring - 1,)),
            sem((ring - 1,)),
            sem((2,)),
            sem((2,)),
        ],
        compiler_params=pltpu.CompilerParams(
            collective_id=0, has_side_effects=True, vmem_limit_bytes=63 << 20
        ),
    )(
        block_io[0], key_code, query_code, attention_gain, attention_shift, triple_bias, output_bias,
        attention_scale, feed_gain, feed_shift, up_bias, down_bias, feed_scale,
        triple_weight[0], output_weight[0], up_weight[0], down_weight[0],
    )
    per = feed // width
    gwd, gwu, gwo, gwt = widened(blocks, width, per)

    flat = vec.reshape(-1)
    vectors = []
    at = 0
    for size in [width] * 8 + [3 * width, feed]:
        vectors.append(flat[at : at + size][None])
        at += size
    ga, gs, gob, gasc, gfg, gfs, gdb, gfsc, gtb, gub = vectors
    return (
        ends[None],
        ga,
        gs,
        gwt[None],
        jnp.concatenate([gtb[:, :width], gtb[:, 2 * width :]], axis=1),
        gwo[None],
        gob,
        gasc,
        gfg,
        gfs,
        gwu[None],
        gub,
        gwd[None],
        gdb,
        gfsc,
    )


def solution(mesh):
    split = ("dp", "inner")
    matrix = P("section", None, None)
    vector = P("section", None)
    return jax.shard_map(
        local,
        mesh=mesh,
        in_specs=(
            P("section", split, None, None), P(split, None), P(split, None),
            vector, vector, matrix, vector, matrix, vector, vector, vector, vector,
            matrix, vector, matrix, vector, vector,
        ),
        out_specs=(
            P("section", split, None, None),
            vector, vector, matrix, vector, matrix, vector, vector, vector, vector,
            matrix, vector, matrix, vector, vector,
        ),
        check_vma=False,
    )
```

```python
import functools

import jax
import jax.numpy as jnp
from jax import lax
from jax.experimental import pallas as pl
from jax.experimental.pallas import tpu as pltpu
from jax.sharding import PartitionSpec as P

HEADS = 12
HEAD = 64
SCALE = HEAD ** (-0.5)
MESH = pl.DeviceIdType.MESH
F32 = jnp.float32
BF16 = jnp.bfloat16
CHUNK = 320
TILE = 768

FWD, DF, DU, DM, ATT, DX, WD, WU, WT = range(9)

NT = (((1,), (1,)), ((), ()))
TN = (((0,), (0,)), ((), ()))


def nt_dot(left, right):
    return lax.dot_general(left, right, NT, preferred_element_type=F32)


def dot(left, right):
    return jnp.dot(left, right, preferred_element_type=F32)


def tn_dot(left, right):
    return lax.dot_general(left, right, TN, preferred_element_type=F32)


def ds(start, size, multiple=None):
    if isinstance(start, int):
        return pl.ds(start, size)
    return pl.ds(pl.multiple_of(start, multiple or size), size)


def standardized(values):
    center = values - jnp.mean(values, axis=-1, keepdims=True)
    spread = jnp.mean(center * center, axis=-1, keepdims=True)
    inverse = lax.rsqrt(spread + 1e-06)
    return center * inverse, inverse


def norm_pull(grad, unit, inverse):
    first = jnp.mean(grad, axis=-1, keepdims=True)
    second = jnp.mean(grad * unit, axis=-1, keepdims=True)
    return inverse * (grad - first - unit * second)


def folded(values):
    rows, columns = values.shape
    return jnp.sum(values.reshape(rows // 8, 8, columns), axis=0)


def gelu_pair(values):
    phi = 0.5 + 0.5 * lax.erf(values * 0.7071067811865476)
    bell = jnp.exp(-0.5 * values * values) * 0.3989422804014327
    return values * phi, phi + values * bell


def picked(table, slot):
    value = jnp.int32(table[0])
    for index in range(1, len(table)):
        if table[index] != table[index - 1]:
            value = jnp.where(slot >= index, jnp.int32(table[index]), value)
    return value


def schedules(count):
    parts = (DF, DU, DM, ATT, DX)
    first = [(FWD, m) for m in range(count)]
    for m in range(count - 1):
        first += [(part, m) for part in parts]
    last = count - 1
    first += [(DF, last), (WD, 0), (DU, last), (WU, 0), (DM, last), (ATT, last), (WT, 0), (DX, last)]
    second = []
    for m in range(count):
        second += [(FWD, m)] + [(part, m) for part in parts]
    second += [(WD, 0), (WU, 0), (WT, 0)]
    return first, second


def tick_plan(slots, per_phase):
    tick, bases, after, starts = 0, [], [], []
    for phase, unused in slots:
        bases.append(tick)
        if phase in (WD, WU, WT):
            starts += [tick + i for i in range(per_phase)]
            tick += per_phase
            after.append(1)
        else:
            after.append(1 if starts and phase != DX else 0)
            tick += after[-1]
    return bases, after, starts, tick


def kernel(
    count, length, width, feed, lines, depth, group,
    data, key_code, query_code, ag, ash, tb, ob, asc, fg, fsh, ub, db, fsc, wt_h, wo_h, wu_h, wd_h,
    ends, blocks, vec,
    wt, wo, wu, wd, x, a, qkv, o, r, m, c, gp, h, f, g, dr, tmp, bias, lse, prm, acc, acc_f, acc_t, lhs,
    part, twin_part, arrived, vpart, vtwin, varrived,
    load_sem, out_sem, send_sem, recv_sem, stage_send, twin_recv,
    sum_send, sum_recv, all_send, all_recv, pair_send, pair_recv, own_sem,
    vsum_send, vsum_recv, vall_send, vall_recv, vpair_send, vpair_recv,
):
    section = lax.axis_index("section")
    leading = section == 0
    trailing = section == 1
    pairs = width // 128
    rows_all = count * length
    half = width // 2
    n_chunks = length // CHUNK

    weight_copies = [
        pltpu.make_async_copy(src, dst, load_sem.at[i])
        for i, (src, dst) in enumerate(((wt_h, wt), (wo_h, wo), (wu_h, wu), (wd_h, wd)))
    ]

    def rows_of(mb):
        return ds(mb * length, length, 64)

    def chunk_rows(mb, i):
        return ds(mb * length + i * CHUNK, CHUNK, CHUNK)

    def load_x(i):
        return pltpu.make_async_copy(data.at[i], x.at[pl.ds(i * length, length)], load_sem.at[4 + i])

    def load_g(i):
        return pltpu.make_async_copy(data.at[i], g.at[pl.ds(i * length, length)], load_sem.at[4 + i])

    def handed(mb):
        return pltpu.make_async_remote_copy(
            src_ref=dr.at[rows_of(mb)], dst_ref=x.at[rows_of(mb)],
            send_sem=send_sem.at[mb], recv_sem=recv_sem.at[mb],
            device_id={"section": 1 - section}, device_id_type=MESH,
        )

    def returned(mb):
        return pltpu.make_async_remote_copy(
            src_ref=g.at[rows_of(mb)], dst_ref=g.at[rows_of(mb)],
            send_sem=send_sem.at[mb], recv_sem=recv_sem.at[mb],
            device_id={"section": 1 - section}, device_id_type=MESH,
        )

    def out_copy(mb):
        return pltpu.make_async_copy(tmp, ends.at[mb], out_sem)

    @pl.when(leading)
    def _():
        for i in range(count):
            load_x(i).start()

    for copy in weight_copies:
        copy.start()

    @pl.when(trailing)
    def _():
        for i in range(count):
            load_g(i).start()

    dp, z = lax.axis_index("dp"), lax.axis_index("inner")
    core, y = dp % 2, dp // 2
    ring = lines * depth
    place = y * depth + jnp.where(y % 2 == 0, z, depth - 1 - z)

    def ring_device(index):
        index = lax.rem(index + ring, ring)
        row, along = index // depth, index % depth
        return {"dp": row * 2 + core, "inner": jnp.where(row % 2 == 0, along, depth - 1 - along)}

    neighbours = (ring_device(place + 1), ring_device(place - 1))
    sibling = {"dp": y * 2 + 1 - core}

    barrier = pltpu.get_barrier_semaphore()
    for device in ({"section": 1 - section}, sibling) + neighbours:
        pl.semaphore_signal(barrier, inc=1, device_id=device, device_id_type=MESH)

    for row, ref in enumerate((ag, ash, ob, asc, fg, fsh, db, fsc)):
        prm[pl.ds(row, 1), pl.ds(0, width)] = ref[...].astype(F32)
    prm[pl.ds(8, 1), pl.ds(0, width)] = tb[:, pl.ds(0, width)].astype(F32)
    prm[pl.ds(8, 1), pl.ds(width, width)] = jnp.zeros((1, width), F32)
    prm[pl.ds(8, 1), pl.ds(2 * width, width)] = tb[:, pl.ds(width, width)].astype(F32)
    prm[pl.ds(9, 1), :] = ub[...].astype(F32)

    def param(row):
        return prm[pl.ds(row, 1), pl.ds(0, width)]

    acc[...] = jnp.zeros_like(acc)
    acc_f[...] = jnp.zeros_like(acc_f)
    acc_t[...] = jnp.zeros_like(acc_t)

    for i in range(count):
        same = key_code[i] == query_code[i]
        own = lax.broadcasted_iota(jnp.int32, (length, length), 0) == lax.broadcasted_iota(
            jnp.int32, (length, length), 1
        )
        banned = jnp.where(same | own, 0.0, -1000000000.0)
        bias[i] = jnp.concatenate([banned, banned], axis=1).astype(BF16)

    pl.semaphore_wait(barrier, 4)

    lane = lax.broadcasted_iota(jnp.int32, (length, 128), 1) < HEAD

    def norm_one(mb):
        def body(i, carry):
            rr = chunk_rows(mb, i)
            unit, unused = standardized(x[rr, :].astype(F32))
            a[rr, :] = (unit * param(0) + param(1)).astype(BF16)
            return carry

        lax.fori_loop(0, n_chunks, body, 0)

    def triple(mb):
        rows = rows_of(mb)

        def body(n, carry):
            cols = ds(n * TILE, TILE)
            qkv[rows, cols] = (dot(a[rows, :], wt[:, cols]) + prm[pl.ds(8, 1), cols]).astype(BF16)
            return carry

        lax.fori_loop(0, 3 * width // TILE, body, 0)

    def two_heads(values):
        zero = jnp.zeros_like(values)
        return jnp.concatenate([jnp.where(lane, values, zero), jnp.where(lane, zero, values)], axis=0)

    def merged(values):
        return jnp.where(lane, values[:length], values[length:])

    def attend(mb):
        rows = rows_of(mb)

        def body(p, carry):
            q = qkv[rows, ds(p * 128, 128)] * SCALE
            k = qkv[rows, ds(width + p * 128, 128)]
            v = qkv[rows, ds(2 * width + p * 128, 128)]
            s = nt_dot(k, two_heads(q)) + bias[mb].astype(F32)
            top = jnp.max(s, axis=0, keepdims=True)
            e = jnp.exp(s - top)
            total = jnp.sum(e, axis=0, keepdims=True)
            lse[mb, p] = top + jnp.log(total)
            prob = (e * (1.0 / total)).astype(BF16)
            o[rows, ds(p * 128, 128)] = merged(tn_dot(prob, v)).astype(BF16)
            return carry

        lax.fori_loop(0, pairs, body, 0)

    def project(mb):
        rows = rows_of(mb)

        def body(n, carry):
            cols = ds(n * TILE, TILE)
            res = dot(o[rows, :], wo[:, cols]) + prm[pl.ds(2, 1), cols]
            r[rows, cols] = res.astype(BF16)
            m[rows, cols] = x[rows, cols].astype(F32) + prm[pl.ds(3, 1), cols] * res
            return carry

        lax.fori_loop(0, width // TILE, body, 0)

    def norm_two(mb):
        def body(i, carry):
            rr = chunk_rows(mb, i)
            unit, unused = standardized(m[rr, :])
            c[rr, :] = (unit * param(4) + param(5)).astype(BF16)
            return carry

        lax.fori_loop(0, n_chunks, body, 0)

    def up(mb):
        rows = rows_of(mb)

        def body(n, carry):
            cols = ds(n * TILE, TILE)
            u = dot(c[rows, :], wu[:, cols]) + prm[pl.ds(9, 1), cols]
            value, slope = gelu_pair(u)
            h[rows, cols] = value.astype(BF16)
            gp[rows, cols] = slope.astype(BF16)
            return carry

        lax.fori_loop(0, feed // TILE, body, 0)

    def down(mb):
        rows = rows_of(mb)

        def body(n, carry):
            cols = ds(n * TILE, TILE)
            res = dot(h[rows, :], wd[:, cols]) + prm[pl.ds(6, 1), cols]
            f[rows, cols] = res.astype(BF16)
            y = m[rows, cols] + prm[pl.ds(7, 1), cols] * res
            tmp[:, cols] = y
            dr[rows, cols] = y.astype(BF16)
            return carry

        lax.fori_loop(0, width // TILE, body, 0)

    def forward(mb):
        def when_first(act):
            pl.when(mb == 0)(act)

        @pl.when(leading & (mb == 0))
        def _():
            for i in range(count):
                load_x(i).wait()

        @pl.when(trailing)
        def _():
            handed(mb).wait_recv()

        norm_one(mb)
        when_first(weight_copies[0].wait)
        triple(mb)
        attend(mb)
        when_first(weight_copies[1].wait)
        project(mb)
        norm_two(mb)
        when_first(weight_copies[2].wait)
        up(mb)
        when_first(weight_copies[3].wait)

        down(mb)

        @pl.when(leading)
        def _():
            handed(mb).start()

        @pl.when(trailing)
        def _():
            out_copy(mb).start()

    def add_acc(row, values):
        acc[row] += folded(values)

    def grad_f(mb):
        @pl.when(leading)
        def _():
            returned(mb).wait_recv()

        @pl.when(trailing & (mb == 0))
        def _():
            for i in range(count):
                load_g(i).wait()

        def body(i, carry):
            rr = chunk_rows(mb, i)
            up_grad = g[rr, :].astype(F32)
            add_acc(7, up_grad * f[rr, :].astype(F32))
            value = (up_grad * param(7)).astype(BF16)
            f[rr, :] = value
            add_acc(6, value.astype(F32))
            return carry

        lax.fori_loop(0, n_chunks, body, 0)

    def grad_u(mb):
        rows = rows_of(mb)

        def body(n, carry):
            cols = ds(n * TILE, TILE)
            value = (nt_dot(f[rows, :], wd[cols, :]) * gp[rows, cols].astype(F32)).astype(BF16)
            gp[rows, cols] = value
            acc_f[:, cols] += folded(value.astype(F32))
            return carry

        lax.fori_loop(0, feed // TILE, body, 0)

    def grad_m(mb):
        rows = rows_of(mb)

        @pl.when(leading & (mb == 0))
        def _():
            for i in range(count):
                handed(i).wait_send()

        @pl.when(trailing | (mb > 0))
        def _():
            out_copy(jnp.where(leading, mb - 1, mb)).wait()

        def first(n, carry):
            cols = ds(n * TILE, TILE)
            tmp[:, cols] = nt_dot(gp[rows, :], wu[cols, :])
            return carry

        lax.fori_loop(0, width // TILE, first, 0)

        def body(i, carry):
            rr = chunk_rows(mb, i)
            grad = tmp[ds(i * CHUNK, CHUNK), :]
            unit, inverse = standardized(m[rr, :])
            add_acc(4, grad * unit)
            add_acc(5, grad)
            total = g[rr, :].astype(F32) + norm_pull(grad * param(4), unit, inverse)
            m[rr, :] = total
            add_acc(3, total * r[rr, :].astype(F32))
            value = (total * param(3)).astype(BF16)
            dr[rr, :] = value
            add_acc(2, value.astype(F32))
            return carry

        lax.fori_loop(0, n_chunks, body, 0)

        def second(n, carry):
            cols = ds(n * TILE, TILE)
            g[rows, cols] = nt_dot(dr[rows, :], wo[cols, :]).astype(BF16)
            return carry

        lax.fori_loop(0, width // TILE, second, 0)

    def grad_attend(mb):
        rows = rows_of(mb)

        def body(p, carry):
            qc, kc, vc = (ds(part * width + p * 128, 128) for part in range(3))
            q = two_heads(qkv[rows, qc] * SCALE)
            do = two_heads(g[rows, qc])
            k, v = qkv[rows, kc], qkv[rows, vc]
            prob = jnp.exp(nt_dot(k, q) + bias[mb].astype(F32) - lse[mb, p])
            dv = dot(prob.astype(BF16), do).astype(BF16)
            dp = nt_dot(v, do)
            inner = jnp.sum(prob * dp, axis=0, keepdims=True)
            grad = (prob * (dp - inner)).astype(BF16)
            dk = dot(grad, q).astype(BF16)
            dq = (merged(tn_dot(grad, k)) * SCALE).astype(BF16)
            qkv[rows, qc] = dq
            qkv[rows, kc] = dk
            qkv[rows, vc] = dv
            acc_t[:, qc] += folded(dq.astype(F32))
            acc_t[:, vc] += folded(dv.astype(F32))
            return carry

        lax.fori_loop(0, pairs, body, 0)

    def grad_x(mb):
        rows = rows_of(mb)

        def first(n, carry):
            cols = ds(n * TILE, TILE)
            tmp[:, cols] = nt_dot(qkv[rows, :], wt[cols, :])
            return carry

        lax.fori_loop(0, width // TILE, first, 0)

        def body(i, carry):
            rr = chunk_rows(mb, i)
            grad = tmp[ds(i * CHUNK, CHUNK), :]
            unit, inverse = standardized(x[rr, :].astype(F32))
            add_acc(0, grad * unit)
            add_acc(1, grad)
            total = m[rr, :] + norm_pull(grad * param(0), unit, inverse)

            @pl.when(leading)
            def _():
                tmp[ds(i * CHUNK, CHUNK), :] = total

            g[rr, :] = total.astype(BF16)
            return carry

        lax.fori_loop(0, n_chunks, body, 0)

        @pl.when(leading)
        def _():
            out_copy(mb).start()

        @pl.when(trailing)
        def _():
            returned(mb).start()

    n_blocks = (3 * width + width + 2 * feed) // width
    pieces = n_blocks // group
    piece_rows = group * half
    chunk = piece_rows // ring
    slots = schedules(count)
    plans = [tick_plan(entry, pieces // 3) for entry in slots]

    def chosen(what, index):
        return jnp.where(leading, picked(plans[0][what], index), picked(plans[1][what], index))

    staged = n_blocks * half

    def remote(src, dst, send, recv, device):
        return pltpu.make_async_remote_copy(
            src_ref=src, dst_ref=dst, send_sem=send, recv_sem=recv, device_id=device, device_id_type=MESH
        )

    def twin_copy(block, slot):
        return remote(
            part.at[ds(staged + slot * half, half, 16)], twin_part.at[ds(block * half, half, 16)],
            stage_send.at[slot], twin_recv.at[block], sibling,
        )

    def half_block(index, source):
        piece, turn = index // (2 * group), index % (2 * group)
        away = turn < group
        block = piece * group + turn % group
        slot = turn % 2
        side = jnp.where(away, 1 - core, core)
        base = pl.multiple_of(jnp.where(away, staged + slot * half, block * half), 16)

        @pl.when(away & ((piece > 0) | (turn > 1)))
        def _():
            twin_copy(block, slot).wait_send()

        source(block, side, base)

        @pl.when(away)
        def _():
            twin_copy(block, slot).start()

    def product(left, right, left_start, right_start, base):
        lhs[...] = left[:, ds(left_start, half, 128)].T

        def tile(n, inner):
            part[pl.ds(base, half), ds(n * TILE, TILE)] = dot(
                lhs[...], right[:, ds(right_start + n * TILE, TILE)]
            ).astype(BF16)
            return inner

        lax.fori_loop(0, width // TILE, tile, 0)

    per = feed // width

    def from_down(block, side, base):
        product(h, f, block * width + side * half, 0, base)

    def from_up(block, side, base):
        product(c, gp, side * half, (block - per) * width, base)

    def from_rest(block, side, base):
        pl.when(block == 2 * per)(lambda: product(o, dr, side * half, 0, base))
        pl.when(block > 2 * per)(lambda: product(a, qkv, side * half, (block - 2 * per - 1) * width, base))

    halves = 2 * per

    def weight_grad(phase, source, base):
        def body(i, carry):
            @pl.when((i > 0) & (lax.rem(i, 2 * group) == 0))
            def _():
                tick(base + i // (2 * group) - 1)

            half_block(phase * halves + i, source)
            return carry

        lax.fori_loop(0, halves, body, 0)

    def where_rows(k, j):
        return ds(k * piece_rows + j * chunk, chunk, 16)

    def where_out(k, j):
        offset = k * piece_rows + j * chunk
        return ds((offset // half) * width + core * half + offset % half, chunk, 16)

    def wrapped(index):
        return lax.rem(index + 2 * ring, ring)

    def sum_copy(k, d, s, j):
        index = (k * 2 + d) * (ring - 1) + s
        return remote(
            part.at[where_rows(k, j), pl.ds(d * half, half)], arrived.at[index],
            sum_send.at[index], sum_recv.at[index], neighbours[d],
        )

    def all_copy(k, d, s, j):
        index = (k * 2 + d) * (ring - 1) + s
        there = blocks.at[where_out(k, j), pl.ds(d * half, half)]
        return remote(there, there, all_send.at[index], all_recv.at[index], neighbours[d])

    def all_first(k, d, j):
        index = (k * 2 + d) * (ring - 1)
        return remote(
            part.at[where_rows(k, j), pl.ds(d * half, half)], blocks.at[where_out(k, j), pl.ds(d * half, half)],
            all_send.at[index], all_recv.at[index], neighbours[d],
        )

    def pair_copy(k, d, src, j):
        index = k * 2 + d
        return remote(
            src, blocks.at[where_out(k, j), pl.ds(d * half, half)], pair_send.at[index], pair_recv.at[index], sibling
        )

    def own_copy(k, d, j):
        return pltpu.make_async_copy(
            part.at[where_rows(k, j), pl.ds(d * half, half)], blocks.at[where_out(k, j), pl.ds(d * half, half)],
            own_sem.at[k * 2 + d],
        )

    def piece_event(k, e):
        @pl.when(e == 0)
        def _():
            for b in range(group):
                twin_copy(k * group + b, 0).wait_recv()

            def combine(i, carry):
                rr = ds(k * piece_rows + i * half, half)
                part[rr, :] = (part[rr, :].astype(F32) + twin_part[rr, :].astype(F32)).astype(BF16)
                return carry

            lax.fori_loop(0, group, combine, 0)
            for d in range(2):
                sum_copy(k, d, 0, place).start()

        @pl.when((e > 0) & (e < ring))
        def _():
            s = e - 1
            for d, sign in ((0, 1), (1, -1)):
                j = wrapped(place - sign * (s + 1))
                sum_copy(k, d, s, j).wait_recv()
                rr, cols = where_rows(k, j), pl.ds(d * half, half)
                total = part[rr, cols].astype(F32) + arrived[(k * 2 + d) * (ring - 1) + s].astype(F32)
                part[rr, cols] = total.astype(BF16)

                @pl.when(e < ring - 1)
                def _():
                    sum_copy(k, d, e, j).start()

                @pl.when(e == ring - 1)
                def _():
                    all_first(k, d, j).start()
                    pair_copy(k, d, part.at[rr, cols], j).start()
                    own_copy(k, d, j).start()

        @pl.when(e >= ring)
        def _():
            s = e - ring
            for d, sign in ((0, 1), (1, -1)):
                j = wrapped(place - sign * s)
                all_copy(k, d, s, j).wait_recv()

                @pl.when(s < ring - 2)
                def _():
                    all_copy(k, d, s + 1, j).start()

                pair_copy(k, d, blocks.at[where_out(k, j), pl.ds(d * half, half)], j).start()

    events = 2 * ring - 1

    def tick(t):
        def body(k, carry):
            e = t - chosen(2, k)
            pl.when((e >= 0) & (e < events))(lambda: piece_event(k, e))
            return carry

        lax.fori_loop(0, pieces, body, 0)

    vhalf = ring * 8

    def vrows(j):
        return ds(core * vhalf + j * 8, 8)

    def vpair_copy():
        return remote(vpart.at[ds((1 - core) * vhalf, vhalf)], vtwin, vpair_send.at[0], vpair_recv.at[0], sibling)

    def vsum_copy(s, j):
        return remote(vpart.at[vrows(j)], varrived.at[s], vsum_send.at[s], vsum_recv.at[s], neighbours[0])

    def vall_copy(s, j, src):
        return remote(src.at[vrows(j)], vec.at[vrows(j)], vall_send.at[s], vall_recv.at[s], neighbours[0])

    def vout_copy(src, rr):
        return remote(src.at[rr], vec.at[rr], vpair_send.at[1], vpair_recv.at[1], sibling)

    def vector_event(e):
        @pl.when(e == 0)
        def _():
            vpair_copy().start()
            vpair_copy().wait_recv()
            rr = ds(core * vhalf, vhalf)
            vpart[rr, :] = vpart[rr, :] + vtwin[...]
            vsum_copy(0, place).start()

        @pl.when((e > 0) & (e < ring))
        def _():
            j = wrapped(place - e)
            vsum_copy(e - 1, j).wait_recv()
            rr = vrows(j)
            vpart[rr, :] = vpart[rr, :] + varrived[e - 1]

            @pl.when(e < ring - 1)
            def _():
                vsum_copy(e, j).start()

            @pl.when(e == ring - 1)
            def _():
                vec[rr, :] = vpart[rr, :]
                vall_copy(0, j, vpart).start()

        @pl.when(e >= ring)
        def _():
            s = e - ring
            j = wrapped(place - s)
            vall_copy(s, j, vec).wait_recv()

            @pl.when(s < ring - 2)
            def _():
                vall_copy(s + 1, j, vec).start()

            @pl.when(s == ring - 2)
            def _():
                vout_copy(vec, ds(core * vhalf, vhalf)).start()

    def pack_vectors():
        vpart[...] = jnp.zeros_like(vpart)
        at = 0
        for ref, size in [(acc.at[row], width) for row in range(8)] + [(acc_t, 3 * width), (acc_f, feed)]:
            for i in range(size // 128):
                vpart[pl.ds(at, 1), :] = jnp.sum(ref[:, pl.ds(i * 128, 128)], axis=0, keepdims=True)
                at += 1

    def finish():
        for d in range(2):
            def body(k, carry):
                whole = blocks.at[ds(k * piece_rows, piece_rows, 16), pl.ds(d * half, half)]
                index = k * 2 + d
                remote(whole, whole, pair_send.at[index], pair_recv.at[index], sibling).wait()
                own_copy(k, d, 0).wait()

                def sends(s, inner):
                    sum_copy(k, d, s, 0).wait_send()
                    all_copy(k, d, s, 0).wait_send()
                    return inner

                return lax.fori_loop(0, ring - 1, sends, carry)

            lax.fori_loop(0, pieces, body, 0)

        def vsends(s, carry):
            vsum_copy(s, 0).wait_send()
            vall_copy(s, 0, vec).wait_send()
            return carry

        lax.fori_loop(0, ring - 1, vsends, 0)
        vpair_copy().wait_send()
        vout_copy(vec, ds(core * vhalf, vhalf)).wait_send()
        vout_copy(vec, ds((1 - core) * vhalf, vhalf)).wait_recv()
        for slot in range(2):
            twin_copy(0, slot).wait_send()

    def slot_body(slot, carry):
        phase = jnp.where(leading, picked([e[0] for e in slots[0]], slot), picked([e[0] for e in slots[1]], slot))
        mb = jnp.where(leading, picked([e[1] for e in slots[0]], slot), picked([e[1] for e in slots[1]], slot))
        base = chosen(0, slot)
        for which, act in ((FWD, forward), (DF, grad_f), (DU, grad_u), (DM, grad_m), (ATT, grad_attend), (DX, grad_x)):
            pl.when(phase == which)(functools.partial(act, mb))
        for number, (which, source) in enumerate(((WD, from_down), (WU, from_up), (WT, from_rest))):
            pl.when(phase == which)(functools.partial(weight_grad, number, source, base))
        inner = jnp.where(phase >= WD, pieces // 3 - 1, 0)
        pl.when(chosen(1, slot) == 1)(lambda: tick(base + inner))
        return carry

    lax.fori_loop(0, len(slots[0]), slot_body, 0)
    pack_vectors()
    start = jnp.where(leading, plans[0][3], plans[1][3])

    def drain(i, carry):
        t = start + i
        tick(t)
        pl.when(i < events)(lambda: vector_event(i))
        return carry

    lax.fori_loop(0, events, drain, 0)
    finish()

    @pl.when(leading)
    def _():
        out_copy(count - 1).wait()

    @pl.when(trailing)
    def _():
        for i in range(count):
            returned(i).wait_send()


def widen_kernel(per, source, gwd, gwu, gwo, gwt):
    block = pl.program_id(0)
    for target, first, after in ((gwd, 0, per), (gwu, per, 2 * per), (gwo, 2 * per, 2 * per + 1), (gwt, 2 * per + 1, 2 * per + 4)):

        @pl.when((block >= first) & (block < after))
        def _():
            target[...] = source[...].astype(F32)


def widened(blocks, width, per):
    def beside(first, number):
        return lambda i: (0, jnp.clip(i - first, 0, number - 1))

    shape = (width, width)
    return pl.pallas_call(
        functools.partial(widen_kernel, per),
        grid=(2 * per + 4,),
        in_specs=[pl.BlockSpec(shape, lambda i: (i, 0))],
        out_specs=(
            pl.BlockSpec(shape, lambda i: (jnp.minimum(i, per - 1), 0)),
            pl.BlockSpec(shape, beside(per, per)),
            pl.BlockSpec(shape, beside(2 * per, 1)),
            pl.BlockSpec(shape, beside(2 * per + 1, 3)),
        ),
        out_shape=(
            jax.ShapeDtypeStruct((per * width, width), F32),
            jax.ShapeDtypeStruct((width, per * width), F32),
            jax.ShapeDtypeStruct((width, width), F32),
            jax.ShapeDtypeStruct((width, 3 * width), F32),
        ),
        compiler_params=pltpu.CompilerParams(vmem_limit_bytes=60 << 20),
    )(blocks)


def local(
    block_io, segments, valid_tokens, attention_gain, attention_shift, triple_weight, triple_bias,
    output_weight, output_bias, attention_scale, feed_gain, feed_shift, up_weight, up_bias,
    down_weight, down_bias, feed_scale,
):
    count, length, width = block_io.shape[1:]
    feed = up_weight.shape[2]
    rows = count * length
    half = width // 2
    lines, depth = lax.axis_size("dp") // 2, lax.axis_size("inner")
    ring = lines * depth
    n_blocks = (4 * width + 2 * feed) // width
    group = 2 if (2 * half) % (16 * ring) == 0 else feed // width
    pieces = n_blocks // group
    streams = pieces * 2 * (ring - 1)
    chunk = group * half // ring
    key_code = jnp.where(valid_tokens == 1, segments, -1)[:, :, None]
    query_code = segments[:, None, :]
    any_spec = pl.BlockSpec(memory_space=pl.ANY)
    vmem = pl.BlockSpec(memory_space=pltpu.VMEM)
    sem = pltpu.SemaphoreType.DMA
    ends, blocks, vec = pl.pallas_call(
        functools.partial(kernel, count, length, width, feed, lines, depth, group),
        out_shape=(
            jax.ShapeDtypeStruct((count, length, width), F32),
            jax.ShapeDtypeStruct((n_blocks * width, width), BF16),
            jax.ShapeDtypeStruct((2 * ring * 8, 128), F32),
        ),
        in_specs=[any_spec] + [vmem] * 12 + [any_spec] * 4,
        out_specs=(any_spec, any_spec, vmem),
        scratch_shapes=[
            pltpu.VMEM((width, 3 * width), BF16),
            pltpu.VMEM((width, width), BF16),
            pltpu.VMEM((width, feed), BF16),
            pltpu.VMEM((feed, width), BF16),
            pltpu.VMEM((rows, width), BF16),
            pltpu.VMEM((rows, width), BF16),
            pltpu.VMEM((rows, 3 * width), BF16),
            pltpu.VMEM((rows, width), BF16),
            pltpu.VMEM((rows, width), BF16),
            pltpu.VMEM((rows, width), F32),
            pltpu.VMEM((rows, width), BF16),
            pltpu.VMEM((rows, feed), BF16),
            pltpu.VMEM((rows, feed), BF16),
            pltpu.VMEM((rows, width), BF16),
            pltpu.VMEM((rows, width), BF16),
            pltpu.VMEM((rows, width), BF16),
            pltpu.VMEM((length, width), F32),
            pltpu.VMEM((count, length, 2 * length), BF16),
            pltpu.VMEM((count, HEADS // 2, 1, 2 * length), F32),
            pltpu.VMEM((16, feed), F32),
            pltpu.VMEM((8, 8, width), F32),
            pltpu.VMEM((8, feed), F32),
            pltpu.VMEM((8, 3 * width), F32),
            pltpu.VMEM((half, rows), BF16),
            pltpu.VMEM((n_blocks * half + 2 * half, width), BF16),
            pltpu.VMEM((n_blocks * half, width), BF16),
            pltpu.VMEM((streams, chunk, half), BF16),
            pltpu.VMEM((2 * ring * 8, 128), F32),
            pltpu.VMEM((ring * 8, 128), F32),
            pltpu.VMEM((ring - 1, 8, 128), F32),
            sem((4 + count,)),
            sem,
            sem((count,)),
            sem((count,)),
            sem((2,)),
            sem((n_blocks,)),
            sem((streams,)),
            sem((streams,)),
            sem((streams,)),
            sem((streams,)),
            sem((2 * pieces,)),
            sem((2 * pieces,)),
            sem((2 * pieces,)),
            sem((ring - 1,)),
            sem((ring - 1,)),
            sem((ring - 1,)),
            sem((ring - 1,)),
            sem((2,)),
            sem((2,)),
        ],
        compiler_params=pltpu.CompilerParams(
            collective_id=0, has_side_effects=True, vmem_limit_bytes=63 << 20
        ),
    )(
        block_io[0], key_code, query_code, attention_gain, attention_shift, triple_bias, output_bias,
        attention_scale, feed_gain, feed_shift, up_bias, down_bias, feed_scale,
        triple_weight[0], output_weight[0], up_weight[0], down_weight[0],
    )
    per = feed // width
    gwd, gwu, gwo, gwt = widened(blocks, width, per)

    flat = vec.reshape(-1)
    vectors = []
    at = 0
    for size in [width] * 8 + [3 * width, feed]:
        vectors.append(flat[at : at + size][None])
        at += size
    ga, gs, gob, gasc, gfg, gfs, gdb, gfsc, gtb, gub = vectors
    return (
        ends[None],
        ga,
        gs,
        gwt[None],
        jnp.concatenate([gtb[:, :width], gtb[:, 2 * width :]], axis=1),
        gwo[None],
        gob,
        gasc,
        gfg,
        gfs,
        gwu[None],
        gub,
        gwd[None],
        gdb,
        gfsc,
    )


def solution(mesh):
    split = ("dp", "inner")
    matrix = P("section", None, None)
    vector = P("section", None)
    return jax.shard_map(
        local,
        mesh=mesh,
        in_specs=(
            P("section", split, None, None), P(split, None), P(split, None),
            vector, vector, matrix, vector, matrix, vector, vector, vector, vector,
            matrix, vector, matrix, vector, vector,
        ),
        out_specs=(
            P("section", split, None, None),
            vector, vector, matrix, vector, matrix, vector, vector, vector, vector,
            matrix, vector, matrix, vector, vector,
        ),
        check_vma=False,
    )
```

```python
import functools

import jax
import jax.numpy as jnp
from jax import lax
from jax.experimental import pallas as pl
from jax.experimental.pallas import tpu as pltpu
from jax.sharding import PartitionSpec as P

HEADS = 12
HEAD = 64
SCALE = HEAD ** (-0.5)
MESH = pl.DeviceIdType.MESH
F32 = jnp.float32
BF16 = jnp.bfloat16
CHUNK = 320
TILE = 768
PAIRS = 6
BACK_PAIRS = 6
WIDE = 3072

FWD, DF, DU, DM, ATT, DX, WD, WU, WT = range(9)

NT = (((1,), (1,)), ((), ()))
TN = (((0,), (0,)), ((), ()))


def nt_dot(left, right):
    return lax.dot_general(left, right, NT, preferred_element_type=F32)


def dot(left, right):
    return jnp.dot(left, right, preferred_element_type=F32)


def tn_dot(left, right):
    return lax.dot_general(left, right, TN, preferred_element_type=F32)


def ds(start, size, multiple=None):
    if isinstance(start, int):
        return pl.ds(start, size)
    return pl.ds(pl.multiple_of(start, multiple or size), size)


def standardized(values):
    center = values - jnp.mean(values, axis=-1, keepdims=True)
    spread = jnp.mean(center * center, axis=-1, keepdims=True)
    inverse = lax.rsqrt(spread + 1e-06)
    return center * inverse, inverse


def norm_pull(grad, unit, inverse):
    first = jnp.mean(grad, axis=-1, keepdims=True)
    second = jnp.mean(grad * unit, axis=-1, keepdims=True)
    return inverse * (grad - first - unit * second)


def folded(values):
    rows, columns = values.shape
    return jnp.sum(values.reshape(rows // 8, 8, columns), axis=0)


def gelu_pair(values):
    phi = 0.5 + 0.5 * lax.erf(values * 0.7071067811865476)
    bell = jnp.exp(-0.5 * values * values) * 0.3989422804014327
    return values * phi, phi + values * bell


def picked(table, slot):
    value = jnp.int32(table[0])
    for index in range(1, len(table)):
        if table[index] != table[index - 1]:
            value = jnp.where(slot >= index, jnp.int32(table[index]), value)
    return value


def schedules(count):
    parts = (DF, DU, DM, ATT, DX)
    first = [(FWD, m) for m in range(count)]
    for m in range(count - 1):
        first += [(part, m) for part in parts]
    last = count - 1
    first += [(DF, last), (WD, 0), (DU, last), (WU, 0), (DM, last), (ATT, last), (WT, 0), (DX, last)]
    second = []
    for m in range(count):
        second += [(FWD, m)] + [(part, m) for part in parts]
    second += [(WD, 0), (WU, 0), (WT, 0)]
    return first, second


def tick_plan(slots, per_phase):
    tick, bases, after, starts = 0, [], [], []
    for phase, unused in slots:
        bases.append(tick)
        if phase in (WD, WU, WT):
            starts += [tick + i for i in range(per_phase)]
            tick += per_phase
            after.append(1)
        else:
            after.append(1 if starts and phase != DX else 0)
            tick += after[-1]
    return bases, after, starts, tick


def kernel(
    count, length, width, feed, lines, depth, group,
    data, segment, valid, ag, ash, tb, ob, asc, fg, fsh, ub, db, fsc, wt_h, wo_h, wu_h, wd_h,
    ends, blocks, vec,
    wt, wo, wu, wd, x, a, qkv, o, r, m, c, gp, h, f, g, dr, tmp, bias, lse, prm, acc, acc_f, acc_t, lhs,
    part, twin_part, arrived, vpart, vtwin, varrived,
    load_sem, out_sem, send_sem, recv_sem, stage_send, twin_recv,
    sum_send, sum_recv, all_send, all_recv, pair_send, pair_recv, own_sem,
    vsum_send, vsum_recv, vall_send, vall_recv, vpair_send, vpair_recv,
):
    section = lax.axis_index("section")
    leading = section == 0
    trailing = section == 1
    pairs = width // 128
    rows_all = count * length
    half = width // 2
    n_chunks = length // CHUNK

    weight_copies = [
        pltpu.make_async_copy(src, dst, load_sem.at[i])
        for i, (src, dst) in enumerate(((wt_h, wt), (wo_h, wo), (wu_h, wu), (wd_h, wd)))
    ]

    def rows_of(mb):
        return ds(mb * length, length, 64)

    def chunk_rows(mb, i):
        return ds(mb * length + i * CHUNK, CHUNK, CHUNK)

    def load_x(i):
        return pltpu.make_async_copy(data.at[i], x.at[pl.ds(i * length, length)], load_sem.at[4 + i])

    def load_g(i):
        return pltpu.make_async_copy(data.at[i], g.at[pl.ds(i * length, length)], load_sem.at[4 + i])

    def handed(mb):
        return pltpu.make_async_remote_copy(
            src_ref=dr.at[rows_of(mb)], dst_ref=x.at[rows_of(mb)],
            send_sem=send_sem.at[mb], recv_sem=recv_sem.at[mb],
            device_id={"section": 1 - section}, device_id_type=MESH,
        )

    def returned(mb):
        return pltpu.make_async_remote_copy(
            src_ref=g.at[rows_of(mb)], dst_ref=g.at[rows_of(mb)],
            send_sem=send_sem.at[mb], recv_sem=recv_sem.at[mb],
            device_id={"section": 1 - section}, device_id_type=MESH,
        )

    def out_copy(mb):
        return pltpu.make_async_copy(tmp, ends.at[mb], out_sem)

    @pl.when(leading)
    def _():
        for i in range(count):
            load_x(i).start()

    for copy in weight_copies:
        copy.start()

    @pl.when(trailing)
    def _():
        for i in range(count):
            load_g(i).start()

    dp, z = lax.axis_index("dp"), lax.axis_index("inner")
    core, y = dp % 2, dp // 2
    ring = lines * depth
    place = y * depth + jnp.where(y % 2 == 0, z, depth - 1 - z)

    def ring_device(index):
        index = lax.rem(index + ring, ring)
        row, along = index // depth, index % depth
        return {"dp": row * 2 + core, "inner": jnp.where(row % 2 == 0, along, depth - 1 - along)}

    neighbours = (ring_device(place + 1), ring_device(place - 1))
    sibling = {"dp": y * 2 + 1 - core}

    barrier = pltpu.get_barrier_semaphore()
    for device in ({"section": 1 - section}, sibling) + neighbours:
        pl.semaphore_signal(barrier, inc=1, device_id=device, device_id_type=MESH)

    for row, ref in enumerate((ag, ash, ob, asc, fg, fsh, db, fsc)):
        prm[pl.ds(row, 1), pl.ds(0, width)] = ref[...].astype(F32)
    prm[pl.ds(8, 1), pl.ds(0, width)] = tb[:, pl.ds(0, width)].astype(F32)
    prm[pl.ds(8, 1), pl.ds(width, width)] = jnp.zeros((1, width), F32)
    prm[pl.ds(8, 1), pl.ds(2 * width, width)] = tb[:, pl.ds(width, width)].astype(F32)
    prm[pl.ds(9, 1), :] = ub[...].astype(F32)

    def param(row):
        return prm[pl.ds(row, 1), pl.ds(0, width)]

    acc[...] = jnp.zeros_like(acc)
    acc_f[...] = jnp.zeros_like(acc_f)
    acc_t[...] = jnp.zeros_like(acc_t)

    for i in range(count):
        number = segment[pl.ds(i, 1), :]
        code = jnp.where(valid[pl.ds(i, 1), :] == 1, number, -1).astype(F32)
        same = jnp.broadcast_to(code, (128, length)).T[:, :1] == number.astype(F32)
        own = lax.broadcasted_iota(jnp.int32, (length, length), 0) == lax.broadcasted_iota(
            jnp.int32, (length, length), 1
        )
        banned = jnp.where(same | own, 0.0, -1000000000.0)
        bias[i] = jnp.concatenate([banned, banned], axis=1).astype(BF16)

    pl.semaphore_wait(barrier, 4)

    lane = lax.broadcasted_iota(jnp.int32, (length, 128), 1) < HEAD

    def norm_one(mb):
        def body(i, carry):
            rr = chunk_rows(mb, i)
            unit, unused = standardized(x[rr, :].astype(F32))
            a[rr, :] = (unit * param(0) + param(1)).astype(BF16)
            return carry

        lax.fori_loop(0, n_chunks, body, 0)

    def triple(mb):
        rows = rows_of(mb)

        def body(n, carry):
            cols = ds(n * 3 * TILE, 3 * TILE)
            qkv[rows, cols] = (dot(a[rows, :], wt[:, cols]) + prm[pl.ds(8, 1), cols]).astype(BF16)
            return carry

        lax.fori_loop(0, width // TILE, body, 0)

    def two_heads(values):
        zero = jnp.zeros_like(values)
        return jnp.concatenate([jnp.where(lane, values, zero), jnp.where(lane, zero, values)], axis=0)

    def merged(values):
        return jnp.where(lane, values[:length], values[length:])

    def attend(mb):
        rows = rows_of(mb)

        def one(p):
            q = qkv[rows, ds(p * 128, 128)] * SCALE
            k = qkv[rows, ds(width + p * 128, 128)]
            v = qkv[rows, ds(2 * width + p * 128, 128)]
            s = nt_dot(k, two_heads(q)) + bias[mb].astype(F32)
            top = jnp.max(s, axis=0, keepdims=True)
            e = jnp.exp(s - top)
            total = jnp.sum(e, axis=0, keepdims=True)
            prob = (e * (1.0 / total)).astype(BF16)
            return top + jnp.log(total), merged(tn_dot(prob, v)).astype(BF16)

        def body(i, carry):
            found = [one(i * PAIRS + b) for b in range(PAIRS)]
            for b, (level, value) in enumerate(found):
                lse[mb, i * PAIRS + b] = level
                o[rows, ds((i * PAIRS + b) * 128, 128)] = value
            return carry

        lax.fori_loop(0, pairs // PAIRS, body, 0)

    def project(mb):
        rows = rows_of(mb)

        def body(n, carry):
            cols = ds(n * TILE, TILE)
            res = dot(o[rows, :], wo[:, cols]) + prm[pl.ds(2, 1), cols]
            r[rows, cols] = res.astype(BF16)
            m[rows, cols] = x[rows, cols].astype(F32) + prm[pl.ds(3, 1), cols] * res
            return carry

        lax.fori_loop(0, width // TILE, body, 0)

    def norm_two(mb):
        def body(i, carry):
            rr = chunk_rows(mb, i)
            unit, unused = standardized(m[rr, :])
            c[rr, :] = (unit * param(4) + param(5)).astype(BF16)
            return carry

        lax.fori_loop(0, n_chunks, body, 0)

    def up(mb):
        rows = rows_of(mb)

        def body(n, carry):
            cols = ds(n * WIDE, WIDE)
            u = dot(c[rows, :], wu[:, cols]) + prm[pl.ds(9, 1), cols]
            value, slope = gelu_pair(u)
            h[rows, cols] = value.astype(BF16)
            gp[rows, cols] = slope.astype(BF16)
            return carry

        lax.fori_loop(0, feed // WIDE, body, 0)

    def down(mb):
        rows = rows_of(mb)

        def body(n, carry):
            cols = ds(n * TILE, TILE)
            res = dot(h[rows, :], wd[:, cols]) + prm[pl.ds(6, 1), cols]
            f[rows, cols] = res.astype(BF16)
            y = m[rows, cols] + prm[pl.ds(7, 1), cols] * res
            tmp[:, cols] = y
            dr[rows, cols] = y.astype(BF16)
            return carry

        lax.fori_loop(0, width // TILE, body, 0)

    def forward(mb):
        def when_first(act):
            pl.when(mb == 0)(act)

        @pl.when(leading & (mb == 0))
        def _():
            for i in range(count):
                load_x(i).wait()

        @pl.when(trailing)
        def _():
            handed(mb).wait_recv()

        norm_one(mb)
        when_first(weight_copies[0].wait)
        triple(mb)
        attend(mb)
        when_first(weight_copies[1].wait)
        project(mb)
        norm_two(mb)
        when_first(weight_copies[2].wait)
        up(mb)
        when_first(weight_copies[3].wait)

        down(mb)

        @pl.when(leading)
        def _():
            handed(mb).start()

        @pl.when(trailing)
        def _():
            out_copy(mb).start()

    def add_acc(row, values):
        acc[row] += folded(values)

    def grad_f(mb):
        @pl.when(leading)
        def _():
            returned(mb).wait_recv()

        @pl.when(trailing & (mb == 0))
        def _():
            for i in range(count):
                load_g(i).wait()

        def body(i, carry):
            rr = chunk_rows(mb, i)
            up_grad = g[rr, :].astype(F32)
            add_acc(7, up_grad * f[rr, :].astype(F32))
            value = (up_grad * param(7)).astype(BF16)
            f[rr, :] = value
            add_acc(6, value.astype(F32))
            return carry

        lax.fori_loop(0, n_chunks, body, 0)

    def grad_u(mb):
        rows = rows_of(mb)

        def body(n, carry):
            cols = ds(n * WIDE, WIDE)
            value = (nt_dot(f[rows, :], wd[cols, :]) * gp[rows, cols].astype(F32)).astype(BF16)
            gp[rows, cols] = value
            acc_f[:, cols] += folded(value.astype(F32))
            return carry

        lax.fori_loop(0, feed // WIDE, body, 0)

    def grad_m(mb):
        rows = rows_of(mb)

        @pl.when(leading & (mb == 0))
        def _():
            for i in range(count):
                handed(i).wait_send()

        @pl.when(trailing | (mb > 0))
        def _():
            out_copy(jnp.where(leading, mb - 1, mb)).wait()

        def first(n, carry):
            cols = ds(n * TILE, TILE)
            tmp[:, cols] = nt_dot(gp[rows, :], wu[cols, :])
            return carry

        lax.fori_loop(0, width // TILE, first, 0)

        def body(i, carry):
            rr = chunk_rows(mb, i)
            grad = tmp[ds(i * CHUNK, CHUNK), :]
            unit, inverse = standardized(m[rr, :])
            add_acc(4, grad * unit)
            add_acc(5, grad)
            total = g[rr, :].astype(F32) + norm_pull(grad * param(4), unit, inverse)
            m[rr, :] = total
            add_acc(3, total * r[rr, :].astype(F32))
            value = (total * param(3)).astype(BF16)
            dr[rr, :] = value
            add_acc(2, value.astype(F32))
            return carry

        lax.fori_loop(0, n_chunks, body, 0)

        def second(n, carry):
            cols = ds(n * TILE, TILE)
            g[rows, cols] = nt_dot(dr[rows, :], wo[cols, :]).astype(BF16)
            return carry

        lax.fori_loop(0, width // TILE, second, 0)

    def grad_attend(mb):
        rows = rows_of(mb)

        def one(p):
            qc, kc, vc = (ds(part * width + p * 128, 128) for part in range(3))
            q = two_heads(qkv[rows, qc] * SCALE)
            do = two_heads(g[rows, qc])
            k, v = qkv[rows, kc], qkv[rows, vc]
            prob = jnp.exp(nt_dot(k, q) + bias[mb].astype(F32) - lse[mb, p])
            dv = dot(prob.astype(BF16), do).astype(BF16)
            dp = nt_dot(v, do)
            inner = jnp.sum(prob * dp, axis=0, keepdims=True)
            grad = (prob * (dp - inner)).astype(BF16)
            dk = dot(grad, q).astype(BF16)
            dq = (merged(tn_dot(grad, k)) * SCALE).astype(BF16)
            return dq, dk, dv

        def body(i, carry):
            found = [one(i * BACK_PAIRS + b) for b in range(BACK_PAIRS)]
            for b, grads in enumerate(found):
                for part, value in enumerate(grads):
                    cols = ds(part * width + (i * BACK_PAIRS + b) * 128, 128)
                    qkv[rows, cols] = value
                    if part != 1:
                        acc_t[:, cols] += folded(value.astype(F32))
            return carry

        lax.fori_loop(0, pairs // BACK_PAIRS, body, 0)

    def grad_x(mb):
        rows = rows_of(mb)

        def first(n, carry):
            cols = ds(n * TILE, TILE)
            tmp[:, cols] = nt_dot(qkv[rows, :], wt[cols, :])
            return carry

        lax.fori_loop(0, width // TILE, first, 0)

        def body(i, carry):
            rr = chunk_rows(mb, i)
            grad = tmp[ds(i * CHUNK, CHUNK), :]
            unit, inverse = standardized(x[rr, :].astype(F32))
            add_acc(0, grad * unit)
            add_acc(1, grad)
            total = m[rr, :] + norm_pull(grad * param(0), unit, inverse)

            @pl.when(leading)
            def _():
                tmp[ds(i * CHUNK, CHUNK), :] = total

            g[rr, :] = total.astype(BF16)
            return carry

        lax.fori_loop(0, n_chunks, body, 0)

        @pl.when(leading)
        def _():
            out_copy(mb).start()

        @pl.when(trailing)
        def _():
            returned(mb).start()

    n_blocks = (3 * width + width + 2 * feed) // width
    pieces = n_blocks // group
    piece_rows = group * half
    chunk = piece_rows // ring
    slots = schedules(count)
    plans = [tick_plan(entry, pieces // 3) for entry in slots]

    def chosen(what, index):
        return jnp.where(leading, picked(plans[0][what], index), picked(plans[1][what], index))

    staged = n_blocks * half

    def remote(src, dst, send, recv, device):
        return pltpu.make_async_remote_copy(
            src_ref=src, dst_ref=dst, send_sem=send, recv_sem=recv, device_id=device, device_id_type=MESH
        )

    def twin_copy(block, slot):
        return remote(
            part.at[ds(staged + slot * half, half, 16)], twin_part.at[ds(block * half, half, 16)],
            stage_send.at[slot], twin_recv.at[block], sibling,
        )

    def half_block(index, source):
        piece, turn = index // (2 * group), index % (2 * group)
        away = turn < group
        block = piece * group + turn % group
        slot = turn % 2
        side = jnp.where(away, 1 - core, core)
        base = pl.multiple_of(jnp.where(away, staged + slot * half, block * half), 16)

        @pl.when(away & ((piece > 0) | (turn > 1)))
        def _():
            twin_copy(block, slot).wait_send()

        source(block, side, base)

        @pl.when(away)
        def _():
            twin_copy(block, slot).start()

    def product(left, right, left_start, right_start, base):
        lhs[...] = left[:, ds(left_start, half, 128)].T

        def tile(n, inner):
            part[pl.ds(base, half), ds(n * TILE, TILE)] = dot(
                lhs[...], right[:, ds(right_start + n * TILE, TILE)]
            ).astype(BF16)
            return inner

        lax.fori_loop(0, width // TILE, tile, 0)

    per = feed // width

    def from_down(block, side, base):
        product(h, f, block * width + side * half, 0, base)

    def from_up(block, side, base):
        product(c, gp, side * half, (block - per) * width, base)

    def from_rest(block, side, base):
        pl.when(block == 2 * per)(lambda: product(o, dr, side * half, 0, base))
        pl.when(block > 2 * per)(lambda: product(a, qkv, side * half, (block - 2 * per - 1) * width, base))

    halves = 2 * per

    def weight_grad(phase, source, base):
        def body(i, carry):
            @pl.when((i > 0) & (lax.rem(i, 2 * group) == 0))
            def _():
                tick(base + i // (2 * group) - 1)

            half_block(phase * halves + i, source)
            return carry

        lax.fori_loop(0, halves, body, 0)

    def where_rows(k, j):
        return ds(k * piece_rows + j * chunk, chunk, 16)

    def where_out(k, j):
        offset = k * piece_rows + j * chunk
        return ds((offset // half) * width + core * half + offset % half, chunk, 16)

    def wrapped(index):
        return lax.rem(index + 2 * ring, ring)

    def sum_copy(k, d, s, j):
        index = (k * 2 + d) * (ring - 1) + s
        return remote(
            part.at[where_rows(k, j), pl.ds(d * half, half)], arrived.at[index],
            sum_send.at[index], sum_recv.at[index], neighbours[d],
        )

    def all_copy(k, d, s, j):
        index = (k * 2 + d) * (ring - 1) + s
        there = blocks.at[where_out(k, j), pl.ds(d * half, half)]
        return remote(there, there, all_send.at[index], all_recv.at[index], neighbours[d])

    def all_first(k, d, j):
        index = (k * 2 + d) * (ring - 1)
        return remote(
            part.at[where_rows(k, j), pl.ds(d * half, half)], blocks.at[where_out(k, j), pl.ds(d * half, half)],
            all_send.at[index], all_recv.at[index], neighbours[d],
        )

    def pair_copy(k, d, src, j):
        index = k * 2 + d
        return remote(
            src, blocks.at[where_out(k, j), pl.ds(d * half, half)], pair_send.at[index], pair_recv.at[index], sibling
        )

    def own_copy(k, d, j):
        return pltpu.make_async_copy(
            part.at[where_rows(k, j), pl.ds(d * half, half)], blocks.at[where_out(k, j), pl.ds(d * half, half)],
            own_sem.at[k * 2 + d],
        )

    def piece_event(k, e):
        @pl.when(e == 0)
        def _():
            for b in range(group):
                twin_copy(k * group + b, 0).wait_recv()

            def combine(i, carry):
                rr = ds(k * piece_rows + i * half, half)
                part[rr, :] = (part[rr, :].astype(F32) + twin_part[rr, :].astype(F32)).astype(BF16)
                return carry

            lax.fori_loop(0, group, combine, 0)
            for d in range(2):
                sum_copy(k, d, 0, place).start()

        @pl.when((e > 0) & (e < ring))
        def _():
            s = e - 1
            for d, sign in ((0, 1), (1, -1)):
                j = wrapped(place - sign * (s + 1))
                sum_copy(k, d, s, j).wait_recv()
                rr, cols = where_rows(k, j), pl.ds(d * half, half)
                total = part[rr, cols].astype(F32) + arrived[(k * 2 + d) * (ring - 1) + s].astype(F32)
                part[rr, cols] = total.astype(BF16)

                @pl.when(e < ring - 1)
                def _():
                    sum_copy(k, d, e, j).start()

                @pl.when(e == ring - 1)
                def _():
                    all_first(k, d, j).start()
                    pair_copy(k, d, part.at[rr, cols], j).start()
                    own_copy(k, d, j).start()

        @pl.when(e >= ring)
        def _():
            s = e - ring
            for d, sign in ((0, 1), (1, -1)):
                j = wrapped(place - sign * s)
                all_copy(k, d, s, j).wait_recv()

                @pl.when(s < ring - 2)
                def _():
                    all_copy(k, d, s + 1, j).start()

                pair_copy(k, d, blocks.at[where_out(k, j), pl.ds(d * half, half)], j).start()

    events = 2 * ring - 1

    def tick(t):
        def body(k, carry):
            e = t - chosen(2, k)
            pl.when((e >= 0) & (e < events))(lambda: piece_event(k, e))
            return carry

        lax.fori_loop(0, pieces, body, 0)

    vhalf = ring * 8

    def vrows(j):
        return ds(core * vhalf + j * 8, 8)

    def vpair_copy():
        return remote(vpart.at[ds((1 - core) * vhalf, vhalf)], vtwin, vpair_send.at[0], vpair_recv.at[0], sibling)

    def vsum_copy(s, j):
        return remote(vpart.at[vrows(j)], varrived.at[s], vsum_send.at[s], vsum_recv.at[s], neighbours[0])

    def vall_copy(s, j, src):
        return remote(src.at[vrows(j)], vec.at[vrows(j)], vall_send.at[s], vall_recv.at[s], neighbours[0])

    def vout_copy(src, rr):
        return remote(src.at[rr], vec.at[rr], vpair_send.at[1], vpair_recv.at[1], sibling)

    def vector_event(e):
        @pl.when(e == 0)
        def _():
            vpair_copy().start()
            vpair_copy().wait_recv()
            rr = ds(core * vhalf, vhalf)
            vpart[rr, :] = vpart[rr, :] + vtwin[...]
            vsum_copy(0, place).start()

        @pl.when((e > 0) & (e < ring))
        def _():
            j = wrapped(place - e)
            vsum_copy(e - 1, j).wait_recv()
            rr = vrows(j)
            vpart[rr, :] = vpart[rr, :] + varrived[e - 1]

            @pl.when(e < ring - 1)
            def _():
                vsum_copy(e, j).start()

            @pl.when(e == ring - 1)
            def _():
                vec[rr, :] = vpart[rr, :]
                vall_copy(0, j, vpart).start()

        @pl.when(e >= ring)
        def _():
            s = e - ring
            j = wrapped(place - s)
            vall_copy(s, j, vec).wait_recv()

            @pl.when(s < ring - 2)
            def _():
                vall_copy(s + 1, j, vec).start()

            @pl.when(s == ring - 2)
            def _():
                vout_copy(vec, ds(core * vhalf, vhalf)).start()

    def pack_vectors():
        vpart[...] = jnp.zeros_like(vpart)
        at = 0
        for ref, size in [(acc.at[row], width) for row in range(8)] + [(acc_t, 3 * width), (acc_f, feed)]:
            for i in range(size // 128):
                vpart[pl.ds(at, 1), :] = jnp.sum(ref[:, pl.ds(i * 128, 128)], axis=0, keepdims=True)
                at += 1

    def finish():
        for d in range(2):
            def body(k, carry):
                whole = blocks.at[ds(k * piece_rows, piece_rows, 16), pl.ds(d * half, half)]
                index = k * 2 + d
                remote(whole, whole, pair_send.at[index], pair_recv.at[index], sibling).wait()
                own_copy(k, d, 0).wait()

                def sends(s, inner):
                    sum_copy(k, d, s, 0).wait_send()
                    all_copy(k, d, s, 0).wait_send()
                    return inner

                return lax.fori_loop(0, ring - 1, sends, carry)

            lax.fori_loop(0, pieces, body, 0)

        def vsends(s, carry):
            vsum_copy(s, 0).wait_send()
            vall_copy(s, 0, vec).wait_send()
            return carry

        lax.fori_loop(0, ring - 1, vsends, 0)
        vpair_copy().wait_send()
        vout_copy(vec, ds(core * vhalf, vhalf)).wait_send()
        vout_copy(vec, ds((1 - core) * vhalf, vhalf)).wait_recv()
        for slot in range(2):
            twin_copy(0, slot).wait_send()

    def slot_body(slot, carry):
        phase = jnp.where(leading, picked([e[0] for e in slots[0]], slot), picked([e[0] for e in slots[1]], slot))
        mb = jnp.where(leading, picked([e[1] for e in slots[0]], slot), picked([e[1] for e in slots[1]], slot))
        base = chosen(0, slot)
        for which, act in ((FWD, forward), (DF, grad_f), (DU, grad_u), (DM, grad_m), (ATT, grad_attend), (DX, grad_x)):
            pl.when(phase == which)(functools.partial(act, mb))
        for number, (which, source) in enumerate(((WD, from_down), (WU, from_up), (WT, from_rest))):
            pl.when(phase == which)(functools.partial(weight_grad, number, source, base))
        inner = jnp.where(phase >= WD, pieces // 3 - 1, 0)
        pl.when(chosen(1, slot) == 1)(lambda: tick(base + inner))
        return carry

    lax.fori_loop(0, len(slots[0]), slot_body, 0)
    pack_vectors()
    start = jnp.where(leading, plans[0][3], plans[1][3])

    def drain(i, carry):
        t = start + i
        tick(t)
        pl.when(i < events)(lambda: vector_event(i))
        return carry

    lax.fori_loop(0, events, drain, 0)
    finish()

    @pl.when(leading)
    def _():
        out_copy(count - 1).wait()

    @pl.when(trailing)
    def _():
        for i in range(count):
            returned(i).wait_send()


def widen_kernel(per, width, feed, depth, source, vec, gwd, gwu, gwo, gwt, *rest):
    vectors, (inside, outside, in_sem, out_sem) = rest[:10], rest[10:]
    half = width // 2
    targets = []
    for block in range(2 * per + 4):
        for part in range(2):
            rows = pl.ds(part * half, half)
            if block < per:
                targets.append(gwd.at[pl.ds(block * width + part * half, half)])
            elif block < 2 * per:
                targets.append(gwu.at[rows, pl.ds((block - per) * width, width)])
            elif block == 2 * per:
                targets.append(gwo.at[rows])
            else:
                targets.append(gwt.at[rows, pl.ds((block - 2 * per - 1) * width, width)])

    def load(index):
        slot = index % depth
        return pltpu.make_async_copy(source.at[pl.ds(index * half, half)], inside.at[slot], in_sem.at[slot])

    def store(index):
        slot = index % depth
        return pltpu.make_async_copy(outside.at[slot], targets[index], out_sem.at[slot])

    count = len(targets)
    for index in range(depth):
        load(index).start()
    at = 0
    for target in vectors:
        for i in range(target.shape[1] // 128):
            if target.shape[1] == 2 * width and i == width // 128:
                at += width // 128
            target[:, pl.ds(i * 128, 128)] = vec[pl.ds(at, 1), :]
            at += 1
    for index in range(count):
        slot = index % depth
        load(index).wait()
        if index >= depth:
            store(index - depth).wait()
        outside[slot] = inside[slot].astype(F32)
        store(index).start()
        if index + depth < count:
            load(index + depth).start()
    for index in range(count - depth, count):
        store(index).wait()


def widened(blocks, vec, width, feed):
    per, depth = feed // width, 6
    any_spec = pl.BlockSpec(memory_space=pl.ANY)
    vmem = pl.BlockSpec(memory_space=pltpu.VMEM)
    sizes = [width] * 8 + [2 * width, feed]
    return pl.pallas_call(
        functools.partial(widen_kernel, per, width, feed, depth),
        in_specs=[any_spec, vmem],
        out_specs=(any_spec,) * 4 + (vmem,) * len(sizes),
        out_shape=(
            jax.ShapeDtypeStruct((per * width, width), F32),
            jax.ShapeDtypeStruct((width, per * width), F32),
            jax.ShapeDtypeStruct((width, width), F32),
            jax.ShapeDtypeStruct((width, 3 * width), F32),
        )
        + tuple(jax.ShapeDtypeStruct((1, size), F32) for size in sizes),
        scratch_shapes=[
            pltpu.VMEM((depth, width // 2, width), BF16),
            pltpu.VMEM((depth, width // 2, width), F32),
            pltpu.SemaphoreType.DMA((depth,)),
            pltpu.SemaphoreType.DMA((depth,)),
        ],
        compiler_params=pltpu.CompilerParams(vmem_limit_bytes=60 << 20),
    )(blocks, vec)


def local(
    block_io, segments, valid_tokens, attention_gain, attention_shift, triple_weight, triple_bias,
    output_weight, output_bias, attention_scale, feed_gain, feed_shift, up_weight, up_bias,
    down_weight, down_bias, feed_scale,
):
    count, length, width = block_io.shape[1:]
    feed = up_weight.shape[2]
    rows = count * length
    half = width // 2
    lines, depth = lax.axis_size("dp") // 2, lax.axis_size("inner")
    ring = lines * depth
    n_blocks = (4 * width + 2 * feed) // width
    group = 2 if (2 * half) % (16 * ring) == 0 else feed // width
    pieces = n_blocks // group
    streams = pieces * 2 * (ring - 1)
    chunk = group * half // ring
    any_spec = pl.BlockSpec(memory_space=pl.ANY)
    vmem = pl.BlockSpec(memory_space=pltpu.VMEM)
    sem = pltpu.SemaphoreType.DMA
    ends, blocks, vec = pl.pallas_call(
        functools.partial(kernel, count, length, width, feed, lines, depth, group),
        out_shape=(
            jax.ShapeDtypeStruct((count, length, width), F32),
            jax.ShapeDtypeStruct((n_blocks * width, width), BF16),
            jax.ShapeDtypeStruct((2 * ring * 8, 128), F32),
        ),
        in_specs=[any_spec] + [vmem] * 12 + [any_spec] * 4,
        out_specs=(any_spec, any_spec, vmem),
        scratch_shapes=[
            pltpu.VMEM((width, 3 * width), BF16),
            pltpu.VMEM((width, width), BF16),
            pltpu.VMEM((width, feed), BF16),
            pltpu.VMEM((feed, width), BF16),
            pltpu.VMEM((rows, width), BF16),
            pltpu.VMEM((rows, width), BF16),
            pltpu.VMEM((rows, 3 * width), BF16),
            pltpu.VMEM((rows, width), BF16),
            pltpu.VMEM((rows, width), BF16),
            pltpu.VMEM((rows, width), F32),
            pltpu.VMEM((rows, width), BF16),
            pltpu.VMEM((rows, feed), BF16),
            pltpu.VMEM((rows, feed), BF16),
            pltpu.VMEM((rows, width), BF16),
            pltpu.VMEM((rows, width), BF16),
            pltpu.VMEM((rows, width), BF16),
            pltpu.VMEM((length, width), F32),
            pltpu.VMEM((count, length, 2 * length), BF16),
            pltpu.VMEM((count, HEADS // 2, 1, 2 * length), F32),
            pltpu.VMEM((16, feed), F32),
            pltpu.VMEM((8, 8, width), F32),
            pltpu.VMEM((8, feed), F32),
            pltpu.VMEM((8, 3 * width), F32),
            pltpu.VMEM((half, rows), BF16),
            pltpu.VMEM((n_blocks * half + 2 * half, width), BF16),
            pltpu.VMEM((n_blocks * half, width), BF16),
            pltpu.VMEM((streams, chunk, half), BF16),
            pltpu.VMEM((2 * ring * 8, 128), F32),
            pltpu.VMEM((ring * 8, 128), F32),
            pltpu.VMEM((ring - 1, 8, 128), F32),
            sem((4 + count,)),
            sem,
            sem((count,)),
            sem((count,)),
            sem((2,)),
            sem((n_blocks,)),
            sem((streams,)),
            sem((streams,)),
            sem((streams,)),
            sem((streams,)),
            sem((2 * pieces,)),
            sem((2 * pieces,)),
            sem((2 * pieces,)),
            sem((ring - 1,)),
            sem((ring - 1,)),
            sem((ring - 1,)),
            sem((ring - 1,)),
            sem((2,)),
            sem((2,)),
        ],
        compiler_params=pltpu.CompilerParams(
            collective_id=0, has_side_effects=True, vmem_limit_bytes=63 << 20
        ),
    )(
        block_io[0], segments, valid_tokens, attention_gain, attention_shift, triple_bias, output_bias,
        attention_scale, feed_gain, feed_shift, up_bias, down_bias, feed_scale,
        triple_weight[0], output_weight[0], up_weight[0], down_weight[0],
    )
    gwd, gwu, gwo, gwt, ga, gs, gob, gasc, gfg, gfs, gdb, gfsc, gtb, gub = widened(blocks, vec, width, feed)
    return (
        ends[None],
        ga,
        gs,
        gwt[None],
        gtb,
        gwo[None],
        gob,
        gasc,
        gfg,
        gfs,
        gwu[None],
        gub,
        gwd[None],
        gdb,
        gfsc,
    )


def solution(mesh):
    split = ("dp", "inner")
    matrix = P("section", None, None)
    vector = P("section", None)
    return jax.shard_map(
        local,
        mesh=mesh,
        in_specs=(
            P("section", split, None, None), P(split, None), P(split, None),
            vector, vector, matrix, vector, matrix, vector, vector, vector, vector,
            matrix, vector, matrix, vector, vector,
        ),
        out_specs=(
            P("section", split, None, None),
            vector, vector, matrix, vector, matrix, vector, vector, vector, vector,
            matrix, vector, matrix, vector, vector,
        ),
        check_vma=False,
    )
```

```python
import functools

import jax
import jax.numpy as jnp
from jax import lax
from jax.experimental import pallas as pl
from jax.experimental.pallas import tpu as pltpu
from jax.sharding import PartitionSpec as P

HEADS = 12
HEAD = 64
SCALE = HEAD ** (-0.5)
MESH = pl.DeviceIdType.MESH
F32 = jnp.float32
BF16 = jnp.bfloat16
CHUNK = 320
TILE = 768
PAIRS = 6
BACK_PAIRS = 6
WIDE = 3072
STEP = 2

FWD, DF, DU, DM, ATT, DX, WD, WU, WT = range(9)

NT = (((1,), (1,)), ((), ()))
TN = (((0,), (0,)), ((), ()))


def nt_dot(left, right):
    return lax.dot_general(left, right, NT, preferred_element_type=F32)


def dot(left, right):
    return jnp.dot(left, right, preferred_element_type=F32)


def tn_dot(left, right):
    return lax.dot_general(left, right, TN, preferred_element_type=F32)


def ds(start, size, multiple=None):
    if isinstance(start, int):
        return pl.ds(start, size)
    return pl.ds(pl.multiple_of(start, multiple or size), size)


def standardized(values):
    center = values - jnp.mean(values, axis=-1, keepdims=True)
    spread = jnp.mean(center * center, axis=-1, keepdims=True)
    inverse = lax.rsqrt(spread + 1e-06)
    return center * inverse, inverse


def norm_pull(grad, unit, inverse):
    first = jnp.mean(grad, axis=-1, keepdims=True)
    second = jnp.mean(grad * unit, axis=-1, keepdims=True)
    return inverse * (grad - first - unit * second)


def folded(values):
    rows, columns = values.shape
    return jnp.sum(values.reshape(rows // 8, 8, columns), axis=0)


def gelu_pair(values):
    phi = 0.5 + 0.5 * lax.erf(values * 0.7071067811865476)
    bell = jnp.exp(-0.5 * values * values) * 0.3989422804014327
    return values * phi, phi + values * bell


def picked(table, slot):
    value = jnp.int32(table[0])
    for index in range(1, len(table)):
        if table[index] != table[index - 1]:
            value = jnp.where(slot >= index, jnp.int32(table[index]), value)
    return value


def schedules(count):
    parts = (DF, DU, DM, ATT, DX)
    first = [(FWD, m) for m in range(count)]
    for m in range(count - 1):
        first += [(part, m) for part in parts]
    last = count - 1
    first += [(DF, last), (WD, 0), (DU, last), (WU, 0), (DM, last), (ATT, last), (WT, 0), (DX, last)]
    second = []
    for m in range(count):
        second += [(FWD, m)] + [(part, m) for part in parts]
    second += [(WD, 0), (WU, 0), (WT, 0)]
    return first, second


def tick_plan(slots, per_phase, turns):
    tick, bases, after, starts = 0, [], [], []
    for phase, unused in slots:
        bases.append(tick)
        if phase in (WD, WU, WT):
            for i in range(per_phase):
                start = tick + (i + 1) * turns // per_phase - 1
                starts.append(start + (start + len(starts)) % 2)
            tick += turns
            after.append(1)
        else:
            after.append(1 if starts and phase != DX else 0)
            tick += after[-1]
    return bases, after, starts, tick


def kernel(
    count, length, width, feed, lines, depth, group,
    data, segment, valid, ag, ash, tb, ob, asc, fg, fsh, ub, db, fsc, wt_h, wo_h, wu_h, wd_h,
    ends, blocks, vec,
    wt, wo, wu, wd, x, a, qkv, o, r, m, c, gp, h, f, g, dr, tmp, bias, lse, prm, acc, acc_f, acc_t, lhs,
    part, twin_part, arrived, vpart, vtwin, varrived,
    load_sem, out_sem, send_sem, recv_sem, stage_send, twin_recv,
    sum_send, sum_recv, all_send, all_recv, pair_send, pair_recv, own_sem,
    vsum_send, vsum_recv, vall_send, vall_recv, vpair_send, vpair_recv,
):
    section = lax.axis_index("section")
    leading = section == 0
    trailing = section == 1
    pairs = width // 128
    rows_all = count * length
    half = width // 2
    n_chunks = length // CHUNK

    weight_copies = [
        pltpu.make_async_copy(src, dst, load_sem.at[i])
        for i, (src, dst) in enumerate(((wt_h, wt), (wo_h, wo), (wu_h, wu), (wd_h, wd)))
    ]

    def rows_of(mb):
        return ds(mb * length, length, 64)

    def chunk_rows(mb, i):
        return ds(mb * length + i * CHUNK, CHUNK, CHUNK)

    def load_x(i):
        return pltpu.make_async_copy(data.at[i], x.at[pl.ds(i * length, length)], load_sem.at[4 + i])

    def load_g(i):
        return pltpu.make_async_copy(data.at[i], g.at[pl.ds(i * length, length)], load_sem.at[4 + i])

    def handed(mb):
        return pltpu.make_async_remote_copy(
            src_ref=dr.at[rows_of(mb)], dst_ref=x.at[rows_of(mb)],
            send_sem=send_sem.at[mb], recv_sem=recv_sem.at[mb],
            device_id={"section": 1 - section}, device_id_type=MESH,
        )

    def returned(mb):
        return pltpu.make_async_remote_copy(
            src_ref=g.at[rows_of(mb)], dst_ref=g.at[rows_of(mb)],
            send_sem=send_sem.at[mb], recv_sem=recv_sem.at[mb],
            device_id={"section": 1 - section}, device_id_type=MESH,
        )

    def out_copy(mb):
        return pltpu.make_async_copy(tmp, ends.at[mb], out_sem)

    @pl.when(leading)
    def _():
        for i in range(count):
            load_x(i).start()

    weight_copies[0].start()

    @pl.when(trailing)
    def _():
        for i in range(count):
            load_g(i).start()

    dp, z = lax.axis_index("dp"), lax.axis_index("inner")
    core, y = dp % 2, dp // 2
    ring = lines * depth
    place = y * depth + jnp.where(y % 2 == 0, z, depth - 1 - z)

    def ring_device(index):
        index = lax.rem(index + ring, ring)
        row, along = index // depth, index % depth
        return {"dp": row * 2 + core, "inner": jnp.where(row % 2 == 0, along, depth - 1 - along)}

    neighbours = (ring_device(place + 1), ring_device(place - 1))
    sibling = {"dp": y * 2 + 1 - core}

    barrier = pltpu.get_barrier_semaphore()
    for device in ({"section": 1 - section}, sibling) + neighbours:
        pl.semaphore_signal(barrier, inc=1, device_id=device, device_id_type=MESH)

    for row, ref in enumerate((ag, ash, ob, asc, fg, fsh, db, fsc)):
        prm[pl.ds(row, 1), pl.ds(0, width)] = ref[...].astype(F32)
    prm[pl.ds(8, 1), pl.ds(0, width)] = tb[:, pl.ds(0, width)].astype(F32)
    prm[pl.ds(8, 1), pl.ds(width, width)] = jnp.zeros((1, width), F32)
    prm[pl.ds(8, 1), pl.ds(2 * width, width)] = tb[:, pl.ds(width, width)].astype(F32)
    prm[pl.ds(9, 1), :] = ub[...].astype(F32)

    def param(row):
        return prm[pl.ds(row, 1), pl.ds(0, width)]

    acc[...] = jnp.zeros_like(acc)
    acc_f[...] = jnp.zeros_like(acc_f)
    acc_t[...] = jnp.zeros_like(acc_t)

    for i in range(count):
        number = segment[pl.ds(i, 1), :]
        code = jnp.where(valid[pl.ds(i, 1), :] == 1, number, -1).astype(F32)
        same = jnp.broadcast_to(code, (128, length)).T[:, :1] == number.astype(F32)
        own = lax.broadcasted_iota(jnp.int32, (length, length), 0) == lax.broadcasted_iota(
            jnp.int32, (length, length), 1
        )
        banned = jnp.where(same | own, 0.0, -1000000000.0)
        bias[i] = jnp.concatenate([banned, banned], axis=1).astype(BF16)


    lane = lax.broadcasted_iota(jnp.int32, (length, 128), 1) < HEAD

    def norm_one(mb):
        def body(i, carry):
            rr = chunk_rows(mb, i)
            unit, unused = standardized(x[rr, :].astype(F32))
            a[rr, :] = (unit * param(0) + param(1)).astype(BF16)
            return carry

        lax.fori_loop(0, n_chunks, body, 0)

    def triple(mb):
        rows = rows_of(mb)

        def body(n, carry):
            cols = ds(n * 3 * TILE, 3 * TILE)
            qkv[rows, cols] = (dot(a[rows, :], wt[:, cols]) + prm[pl.ds(8, 1), cols]).astype(BF16)
            return carry

        lax.fori_loop(0, width // TILE, body, 0)

    def two_heads(values):
        zero = jnp.zeros_like(values)
        return jnp.concatenate([jnp.where(lane, values, zero), jnp.where(lane, zero, values)], axis=0)

    def merged(values):
        return jnp.where(lane, values[:length], values[length:])

    def attend(mb):
        rows = rows_of(mb)

        def one(p):
            q = qkv[rows, ds(p * 128, 128)] * SCALE
            k = qkv[rows, ds(width + p * 128, 128)]
            v = qkv[rows, ds(2 * width + p * 128, 128)]
            s = nt_dot(k, two_heads(q)) + bias[mb].astype(F32)
            top = jnp.max(s, axis=0, keepdims=True)
            e = jnp.exp(s - top)
            total = jnp.sum(e, axis=0, keepdims=True)
            prob = (e * (1.0 / total)).astype(BF16)
            return top + jnp.log(total), merged(tn_dot(prob, v)).astype(BF16)

        def body(i, carry):
            found = [one(i * PAIRS + b) for b in range(PAIRS)]
            for b, (level, value) in enumerate(found):
                lse[mb, i * PAIRS + b] = level
                o[rows, ds((i * PAIRS + b) * 128, 128)] = value
            return carry

        lax.fori_loop(0, pairs // PAIRS, body, 0)

    def project(mb):
        rows = rows_of(mb)

        def body(n, carry):
            cols = ds(n * TILE, TILE)
            res = dot(o[rows, :], wo[:, cols]) + prm[pl.ds(2, 1), cols]
            r[rows, cols] = res.astype(BF16)
            m[rows, cols] = x[rows, cols].astype(F32) + prm[pl.ds(3, 1), cols] * res
            return carry

        lax.fori_loop(0, width // TILE, body, 0)

    def norm_two(mb):
        def body(i, carry):
            rr = chunk_rows(mb, i)
            unit, unused = standardized(m[rr, :])
            c[rr, :] = (unit * param(4) + param(5)).astype(BF16)
            return carry

        lax.fori_loop(0, n_chunks, body, 0)

    def up(mb):
        rows = rows_of(mb)

        def body(n, carry):
            cols = ds(n * WIDE, WIDE)
            u = dot(c[rows, :], wu[:, cols]) + prm[pl.ds(9, 1), cols]
            value, slope = gelu_pair(u)
            h[rows, cols] = value.astype(BF16)
            gp[rows, cols] = slope.astype(BF16)
            return carry

        lax.fori_loop(0, feed // WIDE, body, 0)

    def down(mb):
        rows = rows_of(mb)

        def body(n, carry):
            cols = ds(n * TILE, TILE)
            res = dot(h[rows, :], wd[:, cols]) + prm[pl.ds(6, 1), cols]
            f[rows, cols] = res.astype(BF16)
            y = m[rows, cols] + prm[pl.ds(7, 1), cols] * res
            tmp[:, cols] = y
            dr[rows, cols] = y.astype(BF16)
            return carry

        lax.fori_loop(0, width // TILE, body, 0)

    def forward(mb):
        def when_first(act):
            pl.when(mb == 0)(act)

        @pl.when(leading & (mb == 0))
        def _():
            for i in range(count):
                load_x(i).wait()

        @pl.when(trailing)
        def _():
            handed(mb).wait_recv()

        norm_one(mb)

        @pl.when(mb == 0)
        def _():
            weight_copies[0].wait()
            for copy in weight_copies[1:]:
                copy.start()

        triple(mb)
        attend(mb)
        when_first(weight_copies[1].wait)
        project(mb)
        norm_two(mb)
        when_first(weight_copies[2].wait)
        up(mb)
        when_first(weight_copies[3].wait)

        down(mb)
        when_first(lambda: pl.semaphore_wait(barrier, 4))

        @pl.when(leading)
        def _():
            handed(mb).start()

        @pl.when(trailing)
        def _():
            out_copy(mb).start()

    def add_acc(row, values):
        acc[row] += folded(values)

    def grad_f(mb):
        @pl.when(leading)
        def _():
            returned(mb).wait_recv()

        @pl.when(trailing & (mb == 0))
        def _():
            for i in range(count):
                load_g(i).wait()

        def body(i, carry):
            rr = chunk_rows(mb, i)
            up_grad = g[rr, :].astype(F32)
            add_acc(7, up_grad * f[rr, :].astype(F32))
            value = (up_grad * param(7)).astype(BF16)
            f[rr, :] = value
            add_acc(6, value.astype(F32))
            return carry

        lax.fori_loop(0, n_chunks, body, 0)

    def grad_u(mb):
        rows = rows_of(mb)

        def body(n, carry):
            cols = ds(n * WIDE, WIDE)
            value = (nt_dot(f[rows, :], wd[cols, :]) * gp[rows, cols].astype(F32)).astype(BF16)
            gp[rows, cols] = value
            acc_f[:, cols] += folded(value.astype(F32))
            return carry

        lax.fori_loop(0, feed // WIDE, body, 0)

    def grad_m(mb):
        rows = rows_of(mb)

        @pl.when(leading & (mb == 0))
        def _():
            for i in range(count):
                handed(i).wait_send()

        @pl.when(trailing | (mb > 0))
        def _():
            out_copy(jnp.where(leading, mb - 1, mb)).wait()

        def first(n, carry):
            cols = ds(n * TILE, TILE)
            tmp[:, cols] = nt_dot(gp[rows, :], wu[cols, :])
            return carry

        lax.fori_loop(0, width // TILE, first, 0)

        def body(i, carry):
            rr = chunk_rows(mb, i)
            grad = tmp[ds(i * CHUNK, CHUNK), :]
            unit, inverse = standardized(m[rr, :])
            add_acc(4, grad * unit)
            add_acc(5, grad)
            total = g[rr, :].astype(F32) + norm_pull(grad * param(4), unit, inverse)
            m[rr, :] = total
            add_acc(3, total * r[rr, :].astype(F32))
            value = (total * param(3)).astype(BF16)
            dr[rr, :] = value
            add_acc(2, value.astype(F32))
            return carry

        lax.fori_loop(0, n_chunks, body, 0)

        def second(n, carry):
            cols = ds(n * TILE, TILE)
            g[rows, cols] = nt_dot(dr[rows, :], wo[cols, :]).astype(BF16)
            return carry

        lax.fori_loop(0, width // TILE, second, 0)

    def grad_attend(mb):
        rows = rows_of(mb)

        def one(p):
            qc, kc, vc = (ds(part * width + p * 128, 128) for part in range(3))
            q = two_heads(qkv[rows, qc] * SCALE)
            do = two_heads(g[rows, qc])
            k, v = qkv[rows, kc], qkv[rows, vc]
            prob = jnp.exp(nt_dot(k, q) + bias[mb].astype(F32) - lse[mb, p])
            dv = dot(prob.astype(BF16), do).astype(BF16)
            dp = nt_dot(v, do)
            inner = jnp.sum(prob * dp, axis=0, keepdims=True)
            grad = (prob * (dp - inner)).astype(BF16)
            dk = dot(grad, q).astype(BF16)
            dq = (merged(tn_dot(grad, k)) * SCALE).astype(BF16)
            return dq, dk, dv

        def body(i, carry):
            found = [one(i * BACK_PAIRS + b) for b in range(BACK_PAIRS)]
            for b, grads in enumerate(found):
                for part, value in enumerate(grads):
                    cols = ds(part * width + (i * BACK_PAIRS + b) * 128, 128)
                    qkv[rows, cols] = value
                    if part != 1:
                        acc_t[:, cols] += folded(value.astype(F32))
            return carry

        lax.fori_loop(0, pairs // BACK_PAIRS, body, 0)

    def grad_x(mb):
        rows = rows_of(mb)

        def first(n, carry):
            cols = ds(n * TILE, TILE)
            tmp[:, cols] = nt_dot(qkv[rows, :], wt[cols, :])
            return carry

        lax.fori_loop(0, width // TILE, first, 0)

        def body(i, carry):
            rr = chunk_rows(mb, i)
            grad = tmp[ds(i * CHUNK, CHUNK), :]
            unit, inverse = standardized(x[rr, :].astype(F32))
            add_acc(0, grad * unit)
            add_acc(1, grad)
            total = m[rr, :] + norm_pull(grad * param(0), unit, inverse)

            @pl.when(leading)
            def _():
                tmp[ds(i * CHUNK, CHUNK), :] = total

            g[rr, :] = total.astype(BF16)
            return carry

        lax.fori_loop(0, n_chunks, body, 0)

        @pl.when(leading)
        def _():
            out_copy(mb).start()

        @pl.when(trailing)
        def _():
            returned(mb).start()

    n_blocks = (3 * width + width + 2 * feed) // width
    pieces = n_blocks // group
    piece_rows = group * half
    chunk = piece_rows // ring
    slots = schedules(count)
    plans = [tick_plan(entry, pieces // 3, 2 * (feed // width) // STEP) for entry in slots]

    def chosen(what, index):
        return jnp.where(leading, picked(plans[0][what], index), picked(plans[1][what], index))

    staged = n_blocks * half

    def remote(src, dst, send, recv, device):
        return pltpu.make_async_remote_copy(
            src_ref=src, dst_ref=dst, send_sem=send, recv_sem=recv, device_id=device, device_id_type=MESH
        )

    def twin_copy(block, slot):
        return remote(
            part.at[ds(staged + slot * half, half, 16)], twin_part.at[ds(block * half, half, 16)],
            stage_send.at[slot], twin_recv.at[block], sibling,
        )

    def half_block(index, source):
        piece, turn = index // (2 * group), index % (2 * group)
        away = turn < group
        block = piece * group + turn % group
        slot = turn % 2
        side = jnp.where(away, 1 - core, core)
        base = pl.multiple_of(jnp.where(away, staged + slot * half, block * half), 16)

        @pl.when(away & ((piece > 0) | (turn > 1)))
        def _():
            twin_copy(block, slot).wait_send()

        source(block, side, base)

        @pl.when(away)
        def _():
            twin_copy(block, slot).start()

    def product(left, right, left_start, right_start, base):
        lhs[...] = left[:, ds(left_start, half, 128)].T

        def tile(n, inner):
            part[pl.ds(base, half), ds(n * TILE, TILE)] = dot(
                lhs[...], right[:, ds(right_start + n * TILE, TILE)]
            ).astype(BF16)
            return inner

        lax.fori_loop(0, width // TILE, tile, 0)

    per = feed // width

    def from_down(block, side, base):
        product(h, f, block * width + side * half, 0, base)

    def from_up(block, side, base):
        product(c, gp, side * half, (block - per) * width, base)

    def from_rest(block, side, base):
        pl.when(block == 2 * per)(lambda: product(o, dr, side * half, 0, base))
        pl.when(block > 2 * per)(lambda: product(a, qkv, side * half, (block - 2 * per - 1) * width, base))

    halves = 2 * per

    def weight_grad(phase, source, base):
        def body(i, carry):
            @pl.when((i > 0) & (lax.rem(i, STEP) == 0))
            def _():
                tick(base + i // STEP - 1)

            half_block(phase * halves + i, source)
            return carry

        lax.fori_loop(0, halves, body, 0)

    def where_rows(k, j):
        return ds(k * piece_rows + j * chunk, chunk, 16)

    def where_out(k, j):
        offset = k * piece_rows + j * chunk
        return ds((offset // half) * width + core * half + offset % half, chunk, 16)

    def wrapped(index):
        return lax.rem(index + 2 * ring, ring)

    def sum_copy(k, d, s, j):
        index = (k * 2 + d) * (ring - 1) + s
        return remote(
            part.at[where_rows(k, j), pl.ds(d * half, half)], arrived.at[index],
            sum_send.at[index], sum_recv.at[index], neighbours[d],
        )

    def all_copy(k, d, s, j):
        index = (k * 2 + d) * (ring - 1) + s
        there = blocks.at[where_out(k, j), pl.ds(d * half, half)]
        return remote(there, there, all_send.at[index], all_recv.at[index], neighbours[d])

    def all_first(k, d, j):
        index = (k * 2 + d) * (ring - 1)
        return remote(
            part.at[where_rows(k, j), pl.ds(d * half, half)], blocks.at[where_out(k, j), pl.ds(d * half, half)],
            all_send.at[index], all_recv.at[index], neighbours[d],
        )

    def pair_copy(k, d, src, j):
        index = k * 2 + d
        return remote(
            src, blocks.at[where_out(k, j), pl.ds(d * half, half)], pair_send.at[index], pair_recv.at[index], sibling
        )

    def own_copy(k, d, j):
        return pltpu.make_async_copy(
            part.at[where_rows(k, j), pl.ds(d * half, half)], blocks.at[where_out(k, j), pl.ds(d * half, half)],
            own_sem.at[k * 2 + d],
        )

    def piece_event(k, e):
        @pl.when(e == 0)
        def _():
            for b in range(group):
                twin_copy(k * group + b, 0).wait_recv()

            def combine(i, carry):
                rr = ds(k * piece_rows + i * half, half)
                part[rr, :] = (part[rr, :].astype(F32) + twin_part[rr, :].astype(F32)).astype(BF16)
                return carry

            lax.fori_loop(0, group, combine, 0)
            for d in range(2):
                sum_copy(k, d, 0, place).start()

        @pl.when((e > 0) & (e < ring))
        def _():
            s = e - 1
            for d, sign in ((0, 1), (1, -1)):
                j = wrapped(place - sign * (s + 1))
                sum_copy(k, d, s, j).wait_recv()
                rr, cols = where_rows(k, j), pl.ds(d * half, half)
                total = part[rr, cols].astype(F32) + arrived[(k * 2 + d) * (ring - 1) + s].astype(F32)
                part[rr, cols] = total.astype(BF16)

                @pl.when(e < ring - 1)
                def _():
                    sum_copy(k, d, e, j).start()

                @pl.when(e == ring - 1)
                def _():
                    all_first(k, d, j).start()
                    pair_copy(k, d, part.at[rr, cols], j).start()
                    own_copy(k, d, j).start()

        @pl.when(e >= ring)
        def _():
            s = e - ring
            for d, sign in ((0, 1), (1, -1)):
                j = wrapped(place - sign * s)
                all_copy(k, d, s, j).wait_recv()

                @pl.when(s < ring - 2)
                def _():
                    all_copy(k, d, s + 1, j).start()

                pair_copy(k, d, blocks.at[where_out(k, j), pl.ds(d * half, half)], j).start()

        for d in range(2):
            pl.when((e > 1) & (e <= ring))(lambda d=d: sum_copy(k, d, e - 2, 0).wait_send())
            pl.when(e > ring)(lambda d=d: all_copy(k, d, e - ring - 1, 0).wait_send())

    events = 2 * ring - 1

    def tick(t):
        def body(k, carry):
            since = t - chosen(2, k)
            e = since // 2
            pl.when((since >= 0) & (since % 2 == 0) & (e < events))(lambda: piece_event(k, e))
            return carry

        lax.fori_loop(0, pieces, body, 0)

    vhalf = ring * 8

    def vrows(j):
        return ds(core * vhalf + j * 8, 8)

    def vpair_copy():
        return remote(vpart.at[ds((1 - core) * vhalf, vhalf)], vtwin, vpair_send.at[0], vpair_recv.at[0], sibling)

    def vsum_copy(s, j):
        return remote(vpart.at[vrows(j)], varrived.at[s], vsum_send.at[s], vsum_recv.at[s], neighbours[0])

    def vall_copy(s, j, src):
        return remote(src.at[vrows(j)], vec.at[vrows(j)], vall_send.at[s], vall_recv.at[s], neighbours[0])

    def vout_copy(src, rr):
        return remote(src.at[rr], vec.at[rr], vpair_send.at[1], vpair_recv.at[1], sibling)

    def vector_event(e):
        @pl.when(e == 0)
        def _():
            vpair_copy().start()
            vpair_copy().wait_recv()
            rr = ds(core * vhalf, vhalf)
            vpart[rr, :] = vpart[rr, :] + vtwin[...]
            vsum_copy(0, place).start()

        @pl.when((e > 0) & (e < ring))
        def _():
            j = wrapped(place - e)
            vsum_copy(e - 1, j).wait_recv()
            rr = vrows(j)
            vpart[rr, :] = vpart[rr, :] + varrived[e - 1]

            @pl.when(e < ring - 1)
            def _():
                vsum_copy(e, j).start()

            @pl.when(e == ring - 1)
            def _():
                vec[rr, :] = vpart[rr, :]
                vall_copy(0, j, vpart).start()

        @pl.when(e >= ring)
        def _():
            s = e - ring
            j = wrapped(place - s)
            vall_copy(s, j, vec).wait_recv()

            @pl.when(s < ring - 2)
            def _():
                vall_copy(s + 1, j, vec).start()

            @pl.when(s == ring - 2)
            def _():
                vout_copy(vec, ds(core * vhalf, vhalf)).start()

    def pack_vectors():
        vpart[...] = jnp.zeros_like(vpart)
        at = 0
        for ref, size in [(acc.at[row], width) for row in range(8)] + [(acc_t, 3 * width), (acc_f, feed)]:
            for i in range(size // 128):
                vpart[pl.ds(at, 1), :] = jnp.sum(ref[:, pl.ds(i * 128, 128)], axis=0, keepdims=True)
                at += 1

    def finish():
        for d in range(2):
            def body(k, carry):
                whole = blocks.at[ds(k * piece_rows, piece_rows, 16), pl.ds(d * half, half)]
                index = k * 2 + d
                remote(whole, whole, pair_send.at[index], pair_recv.at[index], sibling).wait()
                own_copy(k, d, 0).wait()

                all_copy(k, d, ring - 2, 0).wait_send()
                return carry

            lax.fori_loop(0, pieces, body, 0)

        def vsends(s, carry):
            vsum_copy(s, 0).wait_send()
            vall_copy(s, 0, vec).wait_send()
            return carry

        lax.fori_loop(0, ring - 1, vsends, 0)
        vpair_copy().wait_send()
        vout_copy(vec, ds(core * vhalf, vhalf)).wait_send()
        vout_copy(vec, ds((1 - core) * vhalf, vhalf)).wait_recv()
        for slot in range(2):
            twin_copy(0, slot).wait_send()

    def slot_body(slot, carry):
        phase = jnp.where(leading, picked([e[0] for e in slots[0]], slot), picked([e[0] for e in slots[1]], slot))
        mb = jnp.where(leading, picked([e[1] for e in slots[0]], slot), picked([e[1] for e in slots[1]], slot))
        base = chosen(0, slot)
        for which, act in ((FWD, forward), (DF, grad_f), (DU, grad_u), (DM, grad_m), (ATT, grad_attend), (DX, grad_x)):
            pl.when(phase == which)(functools.partial(act, mb))
        for number, (which, source) in enumerate(((WD, from_down), (WU, from_up), (WT, from_rest))):
            pl.when(phase == which)(functools.partial(weight_grad, number, source, base))
        inner = jnp.where(phase >= WD, halves // STEP - 1, 0)
        pl.when(chosen(1, slot) == 1)(lambda: tick(base + inner))
        return carry

    lax.fori_loop(0, len(slots[0]), slot_body, 0)
    pack_vectors()
    start = jnp.where(leading, plans[0][3], plans[1][3])

    def drain(i, carry):
        t = start + i
        tick(t)
        pl.when(i % 2 == 0)(lambda: vector_event(i // 2))
        return carry

    lax.fori_loop(0, 2 * events, drain, 0)
    finish()

    @pl.when(leading)
    def _():
        out_copy(count - 1).wait()

    @pl.when(trailing)
    def _():
        for i in range(count):
            returned(i).wait_send()


def widen_kernel(per, width, feed, depth, source, vec, gwd, gwu, gwo, gwt, *rest):
    vectors, (inside, outside, in_sem, out_sem) = rest[:10], rest[10:]
    half = width // 2
    targets = []
    for block in range(2 * per + 4):
        for part in range(2):
            rows = pl.ds(part * half, half)
            if block < per:
                targets.append(gwd.at[pl.ds(block * width + part * half, half)])
            elif block < 2 * per:
                targets.append(gwu.at[rows, pl.ds((block - per) * width, width)])
            elif block == 2 * per:
                targets.append(gwo.at[rows])
            else:
                targets.append(gwt.at[rows, pl.ds((block - 2 * per - 1) * width, width)])

    def load(index):
        slot = index % depth
        return pltpu.make_async_copy(source.at[pl.ds(index * half, half)], inside.at[slot], in_sem.at[slot])

    def store(index):
        slot = index % depth
        return pltpu.make_async_copy(outside.at[slot], targets[index], out_sem.at[slot])

    count = len(targets)
    for index in range(depth):
        load(index).start()
    at = 0
    for target in vectors:
        for i in range(target.shape[1] // 128):
            if target.shape[1] == 2 * width and i == width // 128:
                at += width // 128
            target[:, pl.ds(i * 128, 128)] = vec[pl.ds(at, 1), :]
            at += 1
    for index in range(count):
        slot = index % depth
        load(index).wait()
        if index >= depth:
            store(index - depth).wait()
        outside[slot] = inside[slot].astype(F32)
        store(index).start()
        if index + depth < count:
            load(index + depth).start()
    for index in range(count - depth, count):
        store(index).wait()


def widened(blocks, vec, width, feed):
    per, depth = feed // width, 6
    any_spec = pl.BlockSpec(memory_space=pl.ANY)
    vmem = pl.BlockSpec(memory_space=pltpu.VMEM)
    sizes = [width] * 8 + [2 * width, feed]
    return pl.pallas_call(
        functools.partial(widen_kernel, per, width, feed, depth),
        in_specs=[any_spec, vmem],
        out_specs=(any_spec,) * 4 + (vmem,) * len(sizes),
        out_shape=(
            jax.ShapeDtypeStruct((per * width, width), F32),
            jax.ShapeDtypeStruct((width, per * width), F32),
            jax.ShapeDtypeStruct((width, width), F32),
            jax.ShapeDtypeStruct((width, 3 * width), F32),
        )
        + tuple(jax.ShapeDtypeStruct((1, size), F32) for size in sizes),
        scratch_shapes=[
            pltpu.VMEM((depth, width // 2, width), BF16),
            pltpu.VMEM((depth, width // 2, width), F32),
            pltpu.SemaphoreType.DMA((depth,)),
            pltpu.SemaphoreType.DMA((depth,)),
        ],
        compiler_params=pltpu.CompilerParams(vmem_limit_bytes=60 << 20),
    )(blocks, vec)


def local(
    block_io, segments, valid_tokens, attention_gain, attention_shift, triple_weight, triple_bias,
    output_weight, output_bias, attention_scale, feed_gain, feed_shift, up_weight, up_bias,
    down_weight, down_bias, feed_scale,
):
    count, length, width = block_io.shape[1:]
    feed = up_weight.shape[2]
    rows = count * length
    half = width // 2
    lines, depth = lax.axis_size("dp") // 2, lax.axis_size("inner")
    ring = lines * depth
    n_blocks = (4 * width + 2 * feed) // width
    group = 2 if (2 * half) % (16 * ring) == 0 else feed // width
    pieces = n_blocks // group
    streams = pieces * 2 * (ring - 1)
    chunk = group * half // ring
    any_spec = pl.BlockSpec(memory_space=pl.ANY)
    vmem = pl.BlockSpec(memory_space=pltpu.VMEM)
    sem = pltpu.SemaphoreType.DMA
    ends, blocks, vec = pl.pallas_call(
        functools.partial(kernel, count, length, width, feed, lines, depth, group),
        out_shape=(
            jax.ShapeDtypeStruct((count, length, width), F32),
            jax.ShapeDtypeStruct((n_blocks * width, width), BF16),
            jax.ShapeDtypeStruct((2 * ring * 8, 128), F32),
        ),
        in_specs=[any_spec] + [vmem] * 12 + [any_spec] * 4,
        out_specs=(any_spec, any_spec, vmem),
        scratch_shapes=[
            pltpu.VMEM((width, 3 * width), BF16),
            pltpu.VMEM((width, width), BF16),
            pltpu.VMEM((width, feed), BF16),
            pltpu.VMEM((feed, width), BF16),
            pltpu.VMEM((rows, width), BF16),
            pltpu.VMEM((rows, width), BF16),
            pltpu.VMEM((rows, 3 * width), BF16),
            pltpu.VMEM((rows, width), BF16),
            pltpu.VMEM((rows, width), BF16),
            pltpu.VMEM((rows, width), F32),
            pltpu.VMEM((rows, width), BF16),
            pltpu.VMEM((rows, feed), BF16),
            pltpu.VMEM((rows, feed), BF16),
            pltpu.VMEM((rows, width), BF16),
            pltpu.VMEM((rows, width), BF16),
            pltpu.VMEM((rows, width), BF16),
            pltpu.VMEM((length, width), F32),
            pltpu.VMEM((count, length, 2 * length), BF16),
            pltpu.VMEM((count, HEADS // 2, 1, 2 * length), F32),
            pltpu.VMEM((16, feed), F32),
            pltpu.VMEM((8, 8, width), F32),
            pltpu.VMEM((8, feed), F32),
            pltpu.VMEM((8, 3 * width), F32),
            pltpu.VMEM((half, rows), BF16),
            pltpu.VMEM((n_blocks * half + 2 * half, width), BF16),
            pltpu.VMEM((n_blocks * half, width), BF16),
            pltpu.VMEM((streams, chunk, half), BF16),
            pltpu.VMEM((2 * ring * 8, 128), F32),
            pltpu.VMEM((ring * 8, 128), F32),
            pltpu.VMEM((ring - 1, 8, 128), F32),
            sem((4 + count,)),
            sem,
            sem((count,)),
            sem((count,)),
            sem((2,)),
            sem((n_blocks,)),
            sem((streams,)),
            sem((streams,)),
            sem((streams,)),
            sem((streams,)),
            sem((2 * pieces,)),
            sem((2 * pieces,)),
            sem((2 * pieces,)),
            sem((ring - 1,)),
            sem((ring - 1,)),
            sem((ring - 1,)),
            sem((ring - 1,)),
            sem((2,)),
            sem((2,)),
        ],
        compiler_params=pltpu.CompilerParams(
            collective_id=0, has_side_effects=True, vmem_limit_bytes=63 << 20
        ),
    )(
        block_io[0], segments, valid_tokens, attention_gain, attention_shift, triple_bias, output_bias,
        attention_scale, feed_gain, feed_shift, up_bias, down_bias, feed_scale,
        triple_weight[0], output_weight[0], up_weight[0], down_weight[0],
    )
    gwd, gwu, gwo, gwt, ga, gs, gob, gasc, gfg, gfs, gdb, gfsc, gtb, gub = widened(blocks, vec, width, feed)
    return (
        ends[None],
        ga,
        gs,
        gwt[None],
        gtb,
        gwo[None],
        gob,
        gasc,
        gfg,
        gfs,
        gwu[None],
        gub,
        gwd[None],
        gdb,
        gfsc,
    )


def solution(mesh):
    split = ("dp", "inner")
    matrix = P("section", None, None)
    vector = P("section", None)
    return jax.shard_map(
        local,
        mesh=mesh,
        in_specs=(
            P("section", split, None, None), P(split, None), P(split, None),
            vector, vector, matrix, vector, matrix, vector, vector, vector, vector,
            matrix, vector, matrix, vector, vector,
        ),
        out_specs=(
            P("section", split, None, None),
            vector, vector, matrix, vector, matrix, vector, vector, vector, vector,
            matrix, vector, matrix, vector, vector,
        ),
        check_vma=False,
    )
```
